32 devices in a mesh: dp: 2 (over core), sp: 16 (over z, y, x).
Axes of the slice: x: 2, y: 2, z: 4, core: 2. Of those that a mesh axis runs over, the one named last changes fastest.
Arguments:
- frames: bfloat16 [32, 256, 1152], P(('dp', 'sp')), may hold values from -6 to 6
- cotangent: bfloat16 [32, 256, 1152], P(('dp', 'sp')), may hold values from -6 to 6
- aspect: int32 [2], P('dp'), may hold values from 0 to 2
- table_index: int32 [2], P('dp'), may hold values from 0 to 3
- noise_level: int32 [2], P('dp'), may hold values from 0 to 999
- labels: int32 [2], P('dp'), may hold values from 0 to 100
- row_table: bfloat16 [4, 32, 1152], replicated, may hold values from -3 to 3
- column_table: bfloat16 [4, 32, 1152], replicated, may hold values from -3 to 3
- class_table: bfloat16 [101, 1152], replicated, may hold values from -6 to 6
- time_first: bfloat16 [256, 1152], replicated, may hold values from -0.5 to 0.5
- time_first_bias: bfloat16 [1152], replicated, may hold values from -1.75 to 1.75
- time_second: bfloat16 [1152, 1152], replicated, may hold values from -0.1875 to 0.1875
- time_second_bias: bfloat16 [1152], replicated, may hold values from -1.75 to 1.75
- modulate: bfloat16 [1152, 13824], P(None, 'sp'), may hold values from -0.1875 to 0.1875
- modulate_bias: bfloat16 [13824], P('sp'), may hold values from -1.75 to 1.75
- spatial_input: bfloat16 [1152, 3456], P('sp'), may hold values from -0.1875 to 0.1875
- spatial_input_bias: bfloat16 [2304], P('sp'), may hold values from -1.75 to 1.75
- spatial_output: bfloat16 [1152, 1152], P('sp'), may hold values from -2 to 2
- spatial_output_bias: bfloat16 [1152], P('sp'), may hold values from -1.75 to 1.75
- spatial_expand: bfloat16 [1152, 4608], P('sp'), may hold values from -0.1875 to 0.1875
- spatial_expand_bias: bfloat16 [4608], P('sp'), may hold values from -1.75 to 1.75
- spatial_reduce: bfloat16 [1152, 4608], P('sp'), may hold values from -0.09375 to 0.09375
- spatial_reduce_bias: bfloat16 [1152], P('sp'), may hold values from -1.75 to 1.75
- temporal_input: bfloat16 [1152, 3456], P('sp'), may hold values from -0.1875 to 0.1875
- temporal_input_bias: bfloat16 [2304], P('sp'), may hold values from -1.75 to 1.75
- temporal_output: bfloat16 [1152, 1152], P('sp'), may hold values from -0.75 to 0.75
- temporal_output_bias: bfloat16 [1152], P('sp'), may hold values from -1.75 to 1.75
- temporal_expand: bfloat16 [1152, 4608], P('sp'), may hold values from -0.1875 to 0.1875
- temporal_expand_bias: bfloat16 [4608], P('sp'), may hold values from -1.75 to 1.75
- temporal_reduce: bfloat16 [1152, 4608], P('sp'), may hold values from -0.09375 to 0.09375
- temporal_reduce_bias: bfloat16 [1152], P('sp'), may hold values from -3 to 3
Outputs:
- activations: bfloat16 [32, 256, 1152], P(('dp', 'sp'))
- input_grad: float32 [32, 256, 1152], P(('dp', 'sp'))
- row_table_grad: float32 [4, 32, 1152], P(None, None, 'sp')
- column_table_grad: float32 [4, 32, 1152], P(None, None, 'sp')
- class_table_grad: float32 [101, 1152], replicated
- time_first_grad: float32 [256, 1152], replicated
- time_first_bias_grad: float32 [1152], replicated
- time_second_grad: float32 [1152, 1152], replicated
- time_second_bias_grad: float32 [1152], replicated
- modulate_grad: float32 [1152, 13824], P(None, 'sp')
- modulate_bias_grad: float32 [13824], P('sp')
- spatial_input_grad: float32 [1152, 3456], P('sp')
- spatial_input_bias_grad: float32 [2304], P('sp')
- spatial_output_grad: float32 [1152, 1152], P('sp')
- spatial_output_bias_grad: float32 [1152], P('sp')
- spatial_expand_grad: float32 [1152, 4608], P('sp')
- spatial_expand_bias_grad: float32 [4608], P('sp')
- spatial_reduce_grad: float32 [1152, 4608], P('sp')
- spatial_reduce_bias_grad: float32 [1152], P('sp')
- temporal_input_grad: float32 [1152, 3456], P('sp')
- temporal_input_bias_grad: float32 [2304], P('sp')
- temporal_output_grad: float32 [1152, 1152], P('sp')
- temporal_output_bias_grad: float32 [1152], P('sp')
- temporal_expand_grad: float32 [1152, 4608], P('sp')
- temporal_expand_bias_grad: float32 [4608], P('sp')
- temporal_reduce_grad: float32 [1152, 4608], P('sp')
- temporal_reduce_bias_grad: float32 [1152], P('sp')
The draws below stay inside these ranges and needn't reach their ends.
Inputs may be any that keep to these rules, and one draw needn't show every extreme that they name: `aspect`: 0: 16 rows of 16 patches; 1: 8 rows of 32; 2: 32 rows of 8.
All inputs are finite; a program needn't handle non-finite values.
Results may differ from the reference program's by a relative error of at most 0.023.
Values may be sent and summed in bfloat16 or wider, within the bound.
No kernel may reach another device: no remote copies, remote signals or barrier semaphores. Data moves between devices by JAX's collectives and lax.ppermute only.
A program may use at most 448 MiB of HBM per device.

```python
import math
import jax
import jax.numpy as jnp
from jax import lax

D = 1152
HEADS = 16
HDIM = 72
FF = 4608
FREQ = 256
NCLASS = 101
SIDE = 16
FRAMES = 16
TABLES = 4
TSTEPS = 1000
P_SIZE = 256
GRID = 32
CLIPS = 2
NFR = 32


def level_of(own_key, extent, cuts, low, high):
    factor_of = 1.0
    for axis_at, blocks in cuts:
        heights = jax.random.uniform(jax.random.fold_in(jax.random.fold_in(own_key, 6), axis_at), (blocks,), jnp.float32, low / len(cuts), high / len(cuts))
        factor_of = factor_of * jnp.repeat(jnp.exp(heights), extent[axis_at] // blocks).reshape((-1,) + (1,) * (len(extent) - 1 - axis_at))
    return factor_of


def normal_values(key, dims, width, reach, pieces=(), kind=jnp.bfloat16):
    array = width * jax.random.normal(key, dims, jnp.float32)
    if pieces:
        array = array * level_of(key, dims, pieces, -0.22, 0.18)
    return jnp.clip(array, -reach, reach).astype(kind)


def setup_inputs(seed: int = 0) -> dict:
    streams_of = jax.random.split(jax.random.key(seed), 32)
    frames = normal_values(streams_of[0], (NFR, P_SIZE, D), 1.0, 6.0, ((0, 32),))
    cotangent = normal_values(streams_of[1], (NFR, P_SIZE, D), 1.0, 6.0, ((0, 32),))
    aspect = jax.random.randint(streams_of[2], (CLIPS,), 0, 3).astype(jnp.int32)
    table_index = jax.random.randint(streams_of[3], (CLIPS,), 0, TABLES).astype(jnp.int32)
    noise_level = jax.random.randint(streams_of[4], (CLIPS,), 0, TSTEPS).astype(jnp.int32)
    labels = jax.random.randint(streams_of[5], (CLIPS,), 0, NCLASS).astype(jnp.int32)
    row_table = normal_values(streams_of[6], (TABLES, GRID, D), 0.5, 3.0)
    column_table = normal_values(streams_of[7], (TABLES, GRID, D), 0.5, 3.0)
    class_table = normal_values(streams_of[8], (NCLASS, D), 1.0, 6.0)
    time_first = normal_values(streams_of[9], (FREQ, D), (FREQ // 2) ** -0.5, 0.5)
    time_first_bias = normal_values(streams_of[10], (D,), 0.3, 1.75)
    time_second = normal_values(streams_of[11], (D, D), D ** -0.5, 0.1875)
    time_second_bias = normal_values(streams_of[12], (D,), 0.3, 1.75)
    modulate = normal_values(streams_of[13], (D, 12 * D), D ** -0.5, 0.1875, ((1, 16),))
    modulate_bias = normal_values(streams_of[14], (12 * D,), 0.3, 1.75, ((0, 16),))
    spatial_input = normal_values(streams_of[15], (D, 3 * D), D ** -0.5, 0.1875, ((0, 16),))
    spatial_input_bias = normal_values(streams_of[16], (2 * D,), 0.3, 1.75, ((0, 16),))
    spatial_output = normal_values(streams_of[17], (D, D), (max(D // 128, 1)) ** -0.5, 2.0, ((0, 16),))
    spatial_output_bias = normal_values(streams_of[18], (D,), 0.3, 1.75, ((0, 16),))
    spatial_expand = normal_values(streams_of[19], (D, FF), D ** -0.5, 0.1875, ((0, 16),))
    spatial_expand_bias = normal_values(streams_of[20], (FF,), 0.3, 1.75, ((0, 16),))
    spatial_reduce = normal_values(streams_of[21], (D, FF), FF ** -0.5, 0.09375, ((0, 16),))
    spatial_reduce_bias = normal_values(streams_of[22], (D,), 0.3, 1.75, ((0, 16),))
    temporal_input = normal_values(streams_of[23], (D, 3 * D), D ** -0.5, 0.1875, ((0, 16),))
    temporal_input_bias = normal_values(streams_of[24], (2 * D,), 0.3, 1.75, ((0, 16),))
    temporal_output = normal_values(streams_of[25], (D, D), (max(D // 16, 1)) ** -0.5, 0.75, ((0, 16),))
    temporal_output_bias = normal_values(streams_of[26], (D,), 0.3, 1.75, ((0, 16),))
    temporal_expand = normal_values(streams_of[27], (D, FF), D ** -0.5, 0.1875, ((0, 16),))
    temporal_expand_bias = normal_values(streams_of[28], (FF,), 0.3, 1.75, ((0, 16),))
    temporal_reduce = normal_values(streams_of[29], (D, FF), FF ** -0.5, 0.09375, ((0, 16),))
    temporal_reduce_bias = normal_values(streams_of[30], (D,), 0.5, 3.0, ((0, 16),))
    return {"frames": frames, "cotangent": cotangent, "aspect": aspect, "table_index": table_index, "noise_level": noise_level, "labels": labels, "row_table": row_table, "column_table": column_table, "class_table": class_table, "time_first": time_first, "time_first_bias": time_first_bias, "time_second": time_second, "time_second_bias": time_second_bias, "modulate": modulate, "modulate_bias": modulate_bias, "spatial_input": spatial_input, "spatial_input_bias": spatial_input_bias, "spatial_output": spatial_output, "spatial_output_bias": spatial_output_bias, "spatial_expand": spatial_expand, "spatial_expand_bias": spatial_expand_bias, "spatial_reduce": spatial_reduce, "spatial_reduce_bias": spatial_reduce_bias, "temporal_input": temporal_input, "temporal_input_bias": temporal_input_bias, "temporal_output": temporal_output, "temporal_output_bias": temporal_output_bias, "temporal_expand": temporal_expand, "temporal_expand_bias": temporal_expand_bias, "temporal_reduce": temporal_reduce, "temporal_reduce_bias": temporal_reduce_bias}


EPSILON = 1e-06
HIGHEST = lax.Precision.HIGHEST

@jax.custom_vjp
def low(v):
    return lax.optimization_barrier(v.astype(jnp.bfloat16)).astype(jnp.float32)

@jax.custom_vjp
def low_back(v):
    return v

def low_keep(v):
    return (low(v), None)

def low_pass(kept, grad):
    return (grad,)

def back_keep(v):
    return (v, None)

def back_low(kept, grad):
    return (low(grad),)
low.defvjp(low_keep, low_pass)
low_back.defvjp(back_keep, back_low)

def layer_norm(values):
    center = values - lax.optimization_barrier(jnp.mean(values, axis=-1, keepdims=True))
    return center * lax.rsqrt(lax.optimization_barrier(jnp.mean(center * center, axis=-1, keepdims=True)) + EPSILON)

def split_heads(values):
    return values.reshape(values.shape[:-1] + (HEADS, HDIM))

def block(inputs, modulation, weights, score_form, mix_form):
    w_input, input_bias, w_output, output_bias, w_expand, expand_bias, w_reduce, reduce_bias = weights
    shift_att, scale_att, gate_att, shift_mlp, scale_mlp, gate_mlp = jnp.split(modulation, 6, axis=-1)
    attn_input = low(layer_norm(inputs) * (1.0 + scale_att) + shift_att)
    projected = jnp.dot(attn_input, w_input, precision=HIGHEST)
    query_rows = low(low_back(projected[..., :D] + input_bias[:D]))
    key_rows = low(low_back(projected[..., D:2 * D]))
    value_rows = low(low_back(projected[..., 2 * D:] + input_bias[D:]))
    scores = jnp.einsum(score_form, split_heads(query_rows), split_heads(key_rows), precision=HIGHEST)
    scores = low_back(scores * HDIM ** (-0.5))
    attn_probs = low(jax.nn.softmax(scores, axis=-1))
    attended = jnp.einsum(mix_form, attn_probs, split_heads(value_rows), precision=HIGHEST)
    attended = low(low_back(attended.reshape(inputs.shape)))
    branch = low_back(jnp.dot(attended, w_output.T, precision=HIGHEST) + output_bias)
    hidden = inputs + gate_att * branch
    mlp_input = low(layer_norm(hidden) * (1.0 + scale_mlp) + shift_mlp)
    expanded = low_back(jnp.dot(mlp_input, w_expand, precision=HIGHEST) + expand_bias)
    activated = low(jax.nn.gelu(expanded, approximate=True))
    reduced = low_back(jnp.dot(activated, w_reduce.T, precision=HIGHEST) + reduce_bias)
    return hidden + gate_mlp * reduced

def layer(frames, aspect, table_index, noise_level, labels, params):
    row_table, column_table, class_table = (params[0], params[1], params[2])
    time_first, time_first_bias, time_second, time_second_bias = (params[3], params[4], params[5], params[6])
    modulate, modulate_bias = (params[7], params[8])
    spatial = params[9:17]
    temporal = params[17:25]
    half = FREQ // 2
    frequency = jnp.exp(-math.log(10000.0) * jnp.arange(half, dtype=jnp.float32) / half)
    angles = noise_level.astype(jnp.float32)[:, None] * frequency[None, :]
    embedding = jnp.concatenate([jnp.cos(angles), jnp.sin(angles)], axis=-1)
    time_hidden = low_back(jnp.dot(low(embedding), time_first, precision=HIGHEST) + time_first_bias)
    time_vector = low_back(jnp.dot(low(jax.nn.silu(time_hidden)), time_second, precision=HIGHEST) + time_second_bias)
    condition = time_vector + class_table[labels]
    modulation = low_back(jnp.dot(low(jax.nn.silu(condition)), modulate, precision=HIGHEST) + modulate_bias)
    row_width = jnp.where(aspect == 0, SIDE, jnp.where(aspect == 1, 2 * SIDE, SIDE // 2)).astype(jnp.int32)
    patches = jnp.arange(P_SIZE, dtype=jnp.int32)
    patch_rows = patches[None, :] // row_width[:, None]
    patch_cols = patches[None, :] % row_width[:, None]
    chosen = table_index.astype(jnp.int32)[:, None]
    positions = row_table[chosen, patch_rows] + column_table[chosen, patch_cols]
    block_input = frames.reshape(CLIPS, FRAMES, P_SIZE, D) + positions[:, None]

    def spatial_clip(item):
        return block(item[0], item[1], spatial, 'bqhd,bkhd->bhqk', 'bhqk,bkhd->bqhd')

    def temporal_clip(item):
        return block(item[0], item[1], temporal, 'qphd,kphd->phqk', 'phqk,kphd->qphd')
    spatial_out = lax.map(jax.checkpoint(spatial_clip), (block_input, modulation[:, :6 * D]))
    between = low(low_back(spatial_out))
    temporal_out = lax.map(jax.checkpoint(temporal_clip), (between, modulation[:, 6 * D:]))
    return low(temporal_out).reshape(NFR, P_SIZE, D)

def reference(frames, cotangent, aspect, table_index, noise_level, labels, row_table, column_table, class_table, time_first, time_first_bias, time_second, time_second_bias, modulate, modulate_bias, spatial_input, spatial_input_bias, spatial_output, spatial_output_bias, spatial_expand, spatial_expand_bias, spatial_reduce, spatial_reduce_bias, temporal_input, temporal_input_bias, temporal_output, temporal_output_bias, temporal_expand, temporal_expand_bias, temporal_reduce, temporal_reduce_bias):
    params = tuple((argument.astype(jnp.float32) for argument in (row_table, column_table, class_table, time_first, time_first_bias, time_second, time_second_bias, modulate, modulate_bias, spatial_input, spatial_input_bias, spatial_output, spatial_output_bias, spatial_expand, spatial_expand_bias, spatial_reduce, spatial_reduce_bias, temporal_input, temporal_input_bias, temporal_output, temporal_output_bias, temporal_expand, temporal_expand_bias, temporal_reduce, temporal_reduce_bias)))

    def forward(inputs, weights):
        return layer(inputs, aspect, table_index, noise_level, labels, weights)
    output, pullback = jax.vjp(forward, frames.astype(jnp.float32), params)
    input_grad, weight_grads = pullback(cotangent.astype(jnp.float32))
    return (output.astype(jnp.bfloat16), input_grad, weight_grads[0], weight_grads[1], weight_grads[2], weight_grads[3], weight_grads[4], weight_grads[5], weight_grads[6], weight_grads[7], weight_grads[8], weight_grads[9], weight_grads[10], weight_grads[11], weight_grads[12], weight_grads[13], weight_grads[14], weight_grads[15], weight_grads[16], weight_grads[17], weight_grads[18], weight_grads[19], weight_grads[20], weight_grads[21], weight_grads[22], weight_grads[23], weight_grads[24])
```

```python
from functools import partial
import math

import jax
import jax.numpy as jnp
from jax import lax
from jax.sharding import PartitionSpec as P

HEADS = 16
HDIM = 72
FREQ = 256
SIDE = 16
FRAMES = 16

EPSILON = 1e-06
HIGHEST = lax.Precision.HIGHEST
BF16 = jnp.bfloat16
F32 = jnp.float32


def layer_norm(values):
    center = values - jnp.mean(values, axis=-1, keepdims=True)
    inverse = lax.rsqrt(jnp.mean(center * center, axis=-1, keepdims=True) + EPSILON)
    return (center * inverse, inverse)


def norm_back(gradient, normed, inverse):
    mean_grad = jnp.mean(gradient, axis=-1, keepdims=True)
    mean_cross = jnp.mean(gradient * normed, axis=-1, keepdims=True)
    return inverse * (gradient - mean_grad - normed * mean_cross)


def project(left_rows, weight):
    return lax.dot_general(
        left_rows,
        weight,
        (((left_rows.ndim - 1,), (0,)), ((), ())),
        preferred_element_type=F32,
    )


def project_rows(left_rows, weight):
    return lax.dot_general(
        left_rows,
        weight,
        (((left_rows.ndim - 1,), (1,)), ((), ())),
        preferred_element_type=F32,
    )


def contract_first(left_rows, right_rows, precision=None):
    return lax.dot_general(
        left_rows,
        right_rows,
        (((0,), (0,)), ((), ())),
        preferred_element_type=F32,
        precision=precision,
    )


def flat(values):
    return values.reshape(-1, values.shape[-1])


def token_sum(values):
    return jnp.sum(flat(values).astype(F32), axis=0)


def flip(values, axis, size, bit):
    return lax.ppermute(values, axis, [(i, i ^ bit) for i in range(size)])


def bits_of(size):
    bits = []
    bit = 1
    while bit < size:
        bits.append(bit)
        bit = bit * 2
    assert bit == size
    return bits


def cube_gather(values, axis, size):
    rank = lax.axis_index(axis)
    held = values[None]
    for bit in bits_of(size):
        other = flip(held, axis, size, bit)
        upper = (rank & bit) != 0
        held = jnp.concatenate(
            [jnp.where(upper, other, held), jnp.where(upper, held, other)], axis=0
        )
    return held


def cube_sum(values, axis, size):
    for bit in bits_of(size):
        values = values + flip(values, axis, size, bit)
    return values


def cube_scatter(values, axis, size):
    rank = lax.axis_index(axis)
    for bit in reversed(bits_of(size)):
        upper = (rank & bit) != 0
        low, high = values[:bit], values[bit:]
        away = jnp.where(upper, low, high)
        kept = jnp.where(upper, high, low)
        values = kept + flip(away, axis, size, bit)
    return values[0]


def attention_scores(query, key, stride):
    scores = jnp.einsum("snhd,smhd->shnm", query, key, preferred_element_type=F32)
    scores = scores * HDIM ** (-0.5)
    if stride > 1:
        count = scores.shape[-1]
        row = lax.broadcasted_iota(jnp.int32, (count, count), 0) % stride
        col = lax.broadcasted_iota(jnp.int32, (count, count), 1) % stride
        scores = jnp.where(row == col, scores, -1e30)
    return scores


def attend(query, key, value, stride):
    scores = attention_scores(query, key, stride)
    row_max = jnp.max(scores, axis=-1, keepdims=True)
    exponent = jnp.exp(scores - row_max)
    row_total = jnp.sum(exponent, axis=-1, keepdims=True)
    probs = (exponent / row_total).astype(BF16)
    mixed = jnp.einsum("shnm,smhd->snhd", probs, value, preferred_element_type=F32)
    return (mixed.astype(BF16), row_max + jnp.log(row_total))


def attend_back(query, key, value, logsum, grad_out, stride):
    scale = HDIM ** (-0.5)
    probs = jnp.exp(attention_scores(query, key, stride) - logsum)
    grad_probs = jnp.einsum("snhd,smhd->shnm", grad_out, value, preferred_element_type=F32)
    inner = jnp.sum(probs * grad_probs, axis=-1, keepdims=True)
    grad_scores = (probs * (grad_probs - inner)).astype(BF16)
    grad_query = (
        jnp.einsum("shnm,smhd->snhd", grad_scores, key, preferred_element_type=F32) * scale
    )
    grad_key = (
        jnp.einsum("shnm,snhd->smhd", grad_scores, query, preferred_element_type=F32) * scale
    )
    grad_value = jnp.einsum(
        "shnm,snhd->smhd", probs.astype(BF16), grad_out, preferred_element_type=F32
    )
    return (grad_query.astype(BF16), grad_key.astype(BF16), grad_value.astype(BF16))


class Layout:
    def __init__(self, mesh):
        self.cores = mesh.shape["dp"]
        self.chips = mesh.shape["sp"]
        self.heads = HEADS // self.cores


def core_total(values, lay):
    total = values.astype(BF16).astype(F32)
    for bit in bits_of(lay.cores):
        total = total + flip(total.astype(BF16), "dp", lay.cores, bit).astype(F32)
    return total


def core_part(values, axis, lay):
    share = values.shape[axis] // lay.cores
    return lax.dynamic_slice_in_dim(values, lax.axis_index("dp") * share, share, axis)


def heads_of(values, sequences, lay):
    return values.reshape(sequences, -1, lay.heads, HDIM)


def block_forward(inputs, modulation, weights, biases, stride, lay):
    w_input, w_output, w_expand, w_reduce = weights
    query_bias, value_bias, output_bias, expand_bias, reduce_bias = biases
    groups, count, width = inputs.shape
    share = width // lay.cores
    shift_att, scale_att, gate_att, shift_mlp, scale_mlp, gate_mlp = jnp.split(
        modulation[:, None, :], 6, axis=-1
    )
    normed_att, inverse_att = layer_norm(inputs)
    attn_input = (normed_att * (1.0 + scale_att) + shift_att).astype(BF16)
    projected = project(attn_input, w_input)
    query = heads_of((projected[..., :share] + query_bias).astype(BF16), groups, lay)
    key = heads_of(projected[..., share : 2 * share].astype(BF16), groups, lay)
    value = heads_of((projected[..., 2 * share :] + value_bias).astype(BF16), groups, lay)
    mixed, logsum = attend(query, key, value, stride)
    attended = mixed.reshape(groups, count, share)
    branch = core_total(project_rows(attended, w_output), lay) + output_bias
    hidden = inputs + gate_att * branch
    normed_mlp, inverse_mlp = layer_norm(hidden)
    mlp_input = (normed_mlp * (1.0 + scale_mlp) + shift_mlp).astype(BF16)
    expanded = project(mlp_input, w_expand) + expand_bias
    activated = jax.nn.gelu(expanded, approximate=True).astype(BF16)
    reduced = core_total(project_rows(activated, w_reduce), lay) + reduce_bias
    output = hidden + gate_mlp * reduced
    kept = (
        normed_att,
        inverse_att,
        attn_input,
        query,
        key,
        value,
        attended,
        logsum,
        branch,
        normed_mlp,
        inverse_mlp,
        mlp_input,
        expanded,
        activated,
        reduced,
    )
    return (output, kept)


def block_backward(gradient, kept, modulation, weights, stride, lay):
    w_input, w_output, w_expand, w_reduce = weights
    (
        normed_att,
        inverse_att,
        attn_input,
        query,
        key,
        value,
        attended,
        logsum,
        branch,
        normed_mlp,
        inverse_mlp,
        mlp_input,
        expanded,
        activated,
        reduced,
    ) = kept
    groups, count, width = gradient.shape
    share = width // lay.cores
    shift_att, scale_att, gate_att, shift_mlp, scale_mlp, gate_mlp = jnp.split(
        modulation[:, None, :], 6, axis=-1
    )
    grad_gate_mlp = jnp.sum(gradient * reduced, axis=1)
    grad_reduced = (gradient * gate_mlp).astype(BF16)
    reduce_grad = contract_first(flat(grad_reduced), flat(activated)).astype(BF16)
    grad_activated = project(grad_reduced, w_reduce)
    gelu_back = jax.vjp(partial(jax.nn.gelu, approximate=True), expanded)[1]
    grad_expanded = gelu_back(grad_activated)[0].astype(BF16)
    expand_grad = contract_first(flat(mlp_input), flat(grad_expanded)).astype(BF16)
    grad_mlp_input = core_total(project_rows(grad_expanded, w_expand), lay)
    grad_scale_mlp = jnp.sum(grad_mlp_input * normed_mlp, axis=1)
    grad_shift_mlp = jnp.sum(grad_mlp_input, axis=1)
    grad_hidden = gradient + norm_back(grad_mlp_input * (1.0 + scale_mlp), normed_mlp, inverse_mlp)
    grad_gate_att = jnp.sum(grad_hidden * branch, axis=1)
    grad_branch = (grad_hidden * gate_att).astype(BF16)
    output_grad = contract_first(flat(grad_branch), flat(attended)).astype(BF16)
    grad_attended = project(grad_branch, w_output).astype(BF16)
    grad_query, grad_key, grad_value = attend_back(
        query, key, value, logsum, heads_of(grad_attended, groups, lay), stride
    )
    grad_query = grad_query.reshape(groups, count, share)
    grad_key = grad_key.reshape(groups, count, share)
    grad_value = grad_value.reshape(groups, count, share)
    grad_projected = jnp.concatenate([grad_query, grad_key, grad_value], axis=-1)
    input_grad = contract_first(flat(attn_input), flat(grad_projected)).astype(BF16)
    grad_attn_input = core_total(project_rows(grad_projected, w_input), lay)
    grad_scale_att = jnp.sum(grad_attn_input * normed_att, axis=1)
    grad_shift_att = jnp.sum(grad_attn_input, axis=1)
    grad_inputs = grad_hidden + norm_back(
        grad_attn_input * (1.0 + scale_att), normed_att, inverse_att
    )
    grad_mod = jnp.concatenate(
        [
            grad_shift_att,
            grad_scale_att,
            grad_gate_att,
            grad_shift_mlp,
            grad_scale_mlp,
            grad_gate_mlp,
        ],
        axis=-1,
    )
    split_biases = (token_sum(grad_query), token_sum(grad_value), token_sum(grad_expanded))
    whole_biases = (token_sum(grad_branch), token_sum(grad_reduced))
    return (
        grad_inputs,
        grad_mod,
        split_biases,
        whole_biases,
        (input_grad, output_grad, expand_grad, reduce_grad),
    )


def shard_parts(w_input, w_output, w_expand, w_reduce, lay):
    rows = w_input.shape[0]
    attention = core_part(w_input.reshape(rows, 3, -1), 2, lay).reshape(rows, -1)
    return (
        attention,
        core_part(w_output, 1, lay),
        core_part(w_expand, 1, lay),
        core_part(w_reduce, 1, lay),
    )


def split_columns(values, widths):
    bounds = []
    offset = 0
    for width in widths[:-1]:
        offset = offset + width
        bounds.append(offset)
    return jnp.split(values, bounds, axis=-1)


def fetch_weights(w_input, w_output, w_expand, w_reduce, lay):
    parts = shard_parts(w_input, w_output, w_expand, w_reduce, lay)
    joined = jnp.concatenate(parts, axis=1)
    whole = lax.all_gather(joined, "sp", axis=0, tiled=True)
    return split_columns(whole, [part.shape[1] for part in parts])


def reduce_weights(grads, lay):
    joined = jnp.concatenate(grads, axis=1)
    summed = lax.psum_scatter(joined, "sp", scatter_dimension=0, tiled=True)
    return split_columns(summed, [grad.shape[1] for grad in grads])


def join_columns(parts, lay):
    g_input, g_output, g_expand, g_reduce = [
        cube_gather(part.astype(BF16), "dp", lay.cores).astype(F32) for part in parts
    ]
    rows = g_output.shape[1]
    thirds = g_input.reshape(lay.cores, rows, 3, -1)
    return (
        jnp.transpose(thirds, (1, 2, 0, 3)).reshape(rows, -1),
        jnp.transpose(g_output, (1, 0, 2)).reshape(rows, -1),
        jnp.transpose(g_expand, (1, 0, 2)).reshape(rows, -1),
        jnp.transpose(g_reduce, (1, 0, 2)).reshape(rows, -1),
    )


def to_positions(values, clips, lay):
    moved = lax.all_to_all(values, "sp", split_axis=1, concat_axis=0, tiled=True)
    moved = moved.reshape(clips, -1, values.shape[-1])
    return cube_gather(moved, "dp", lay.cores).reshape(-1, moved.shape[1], moved.shape[2])


def own_group(values, lay):
    share = values.shape[0] // lay.cores
    return lax.dynamic_slice_in_dim(values, lax.axis_index("dp") * share, share, 0)


def to_frames(values, frames_here, lay):
    own = own_group(values, lay)
    own = own.reshape(frames_here * lay.chips, -1, values.shape[-1])
    return lax.all_to_all(own, "sp", split_axis=0, concat_axis=1, tiled=True)


def place_split(values, lay):
    whole = jnp.zeros((lay.cores,) + values.shape, values.dtype)
    whole = lax.dynamic_update_index_in_dim(whole, values, lax.axis_index("dp"), 0)
    return whole.reshape(-1)


def per_device(
    lay,
    frames,
    cotangent,
    aspect,
    table_index,
    noise_level,
    labels,
    row_table,
    column_table,
    class_table,
    time_first,
    time_first_bias,
    time_second,
    time_second_bias,
    modulate,
    modulate_bias,
    spatial_input,
    spatial_input_bias,
    spatial_output,
    spatial_output_bias,
    spatial_expand,
    spatial_expand_bias,
    spatial_reduce,
    spatial_reduce_bias,
    temporal_input,
    temporal_input_bias,
    temporal_output,
    temporal_output_bias,
    temporal_expand,
    temporal_expand_bias,
    temporal_reduce,
    temporal_reduce_bias,
):
    cores, chips = lay.cores, lay.chips
    chip = lax.axis_index("sp")
    core = lax.axis_index("dp")
    frame_count, patches, width = frames.shape
    clips_here = aspect.shape[0]
    clips = cores * clips_here
    clip_here = chip * frame_count // FRAMES

    spatial_weights = fetch_weights(
        spatial_input, spatial_output, spatial_expand, spatial_reduce, lay
    )
    temporal_weights = fetch_weights(
        temporal_input, temporal_output, temporal_expand, temporal_reduce, lay
    )

    facts = cube_gather(jnp.stack([aspect, table_index, noise_level, labels]), "dp", cores)
    group_aspect, group_table = (
        lax.dynamic_index_in_dim(facts[:, k], clip_here, 1, keepdims=False) for k in (0, 1)
    )
    all_levels = facts[:, 2].reshape(clips)
    all_labels = facts[:, 3].reshape(clips)
    group_clips = jnp.arange(cores) * clips_here + clip_here

    half = FREQ // 2
    frequency = jnp.exp(-math.log(10000.0) * jnp.arange(half, dtype=F32) / half)
    angles = all_levels.astype(F32)[:, None] * frequency[None, :]
    embedding = jnp.concatenate([jnp.cos(angles), jnp.sin(angles)], axis=-1).astype(BF16)
    time_hidden = project(embedding, time_first) + time_first_bias.astype(F32)
    time_act = jax.nn.silu(time_hidden).astype(BF16)
    class_pick = (all_labels[:, None] == lax.iota(jnp.int32, class_table.shape[0])[None, :]).astype(
        BF16
    )
    condition = (
        project(time_act, time_second)
        + time_second_bias.astype(F32)
        + project(class_pick, class_table)
    )
    condition_act = jax.nn.silu(condition).astype(BF16)
    mod_cols = project(condition_act, modulate) + modulate_bias.astype(F32)

    bias_shards = (
        spatial_input_bias,
        spatial_output_bias,
        spatial_expand_bias,
        spatial_reduce_bias,
        temporal_input_bias,
        temporal_output_bias,
        temporal_expand_bias,
        temporal_reduce_bias,
    )
    bias_sizes = [shard.shape[0] for shard in bias_shards]
    small = jnp.concatenate([mod_cols.reshape(-1)] + [shard.astype(F32) for shard in bias_shards])
    gathered = cube_gather(small, "sp", chips)
    mod_size = mod_cols.shape[1]
    pieces = split_columns(gathered, [clips * mod_size] + bias_sizes)
    modulation = jnp.transpose(pieces[0].reshape(chips, clips, mod_size), (1, 0, 2)).reshape(
        clips, chips * mod_size
    )
    whole_biases = [piece.reshape(-1) for piece in pieces[1:]]

    def block_biases(parts):
        query_bias, value_bias = jnp.split(parts[0], 2)
        return (
            core_part(query_bias, 0, lay),
            core_part(value_bias, 0, lay),
            parts[1],
            core_part(parts[2], 0, lay),
            parts[3],
        )

    spatial_biases = block_biases(whole_biases[:4])
    temporal_biases = block_biases(whole_biases[4:])
    clip_pick = (group_clips[:, None] == jnp.arange(clips)[None, :]).astype(F32)
    spatial_mod = jnp.sum(
        clip_pick[:, :, None] * modulation[None, :, : 6 * width], axis=1
    )
    temporal_mod = modulation[:, 6 * width :]

    row_width = jnp.where(
        group_aspect == 0, SIDE, jnp.where(group_aspect == 1, 2 * SIDE, SIDE // 2)
    )[:, None, None]
    patch_ids = lax.iota(jnp.int32, patches)[None, :, None]
    grid_ids = lax.iota(jnp.int32, 2 * SIDE)[None, None, :]
    row_pick = (patch_ids // row_width == grid_ids).astype(BF16)
    col_pick = (patch_ids % row_width == grid_ids).astype(BF16)
    row_chosen = jnp.take(row_table, group_table, axis=0)
    col_chosen = jnp.take(column_table, group_table, axis=0)
    positions = jnp.einsum(
        "gpr,grd->gpd", row_pick, row_chosen, preferred_element_type=F32
    ) + jnp.einsum("gpr,grd->gpd", col_pick, col_chosen, preferred_element_type=F32)
    all_frames = cube_gather(frames, "dp", cores).astype(F32)
    block_input = (all_frames + positions[:, None]).reshape(-1, patches, width)
    frame_mod = jnp.repeat(spatial_mod, frame_count, axis=0)

    spatial_out, spatial_kept = block_forward(
        block_input, frame_mod, spatial_weights, spatial_biases, 1, lay
    )
    own_out = own_group(spatial_out.astype(BF16), lay)
    between = to_positions(own_out, clips_here, lay)
    local_patches = patches // chips
    temporal_out, temporal_kept = block_forward(
        between.astype(F32), temporal_mod, temporal_weights, temporal_biases, local_patches, lay
    )
    activations = to_frames(temporal_out.astype(BF16), frame_count, lay)
    grad_after = to_positions(cotangent, clips_here, lay)
    grad_between, temporal_dmod, temporal_split, temporal_whole, temporal_grads = block_backward(
        grad_after.astype(F32), temporal_kept, temporal_mod, temporal_weights, local_patches, lay
    )
    temporal_sums = reduce_weights(temporal_grads, lay)
    own_grad = to_frames(grad_between.astype(BF16), frame_count, lay)
    grad_frames = cube_gather(own_grad, "dp", cores).reshape(-1, patches, width)
    input_grad_all, frame_dmod, spatial_split, spatial_whole, spatial_grads = block_backward(
        grad_frames.astype(F32), spatial_kept, frame_mod, spatial_weights, 1, lay
    )
    spatial_sums = reduce_weights(spatial_grads, lay)
    input_grad = own_group(input_grad_all, lay)

    grad_positions = jnp.sum(input_grad, axis=0)
    own_rows = lax.dynamic_index_in_dim(row_pick, core, 0, keepdims=False).astype(F32)
    own_cols = lax.dynamic_index_in_dim(col_pick, core, 0, keepdims=False).astype(F32)
    table_part = contract_first(
        jnp.concatenate([own_rows, own_cols], axis=1), grad_positions, HIGHEST
    )
    here = (lax.iota(jnp.int32, clips_here) == clip_here).astype(F32)
    table_part = here[:, None, None] * table_part[None]

    spatial_dmod = jnp.sum(frame_dmod.reshape(cores, frame_count, -1), axis=1)
    spatial_dmod = jnp.sum(clip_pick[:, :, None] * spatial_dmod[:, None, :], axis=0)
    grad_mod = jnp.concatenate([spatial_dmod, temporal_dmod], axis=-1)

    def by_chip(values):
        parts = values.reshape(-1, chips, values.shape[-1] // chips)
        return jnp.transpose(parts, (1, 0, 2)).reshape(chips, -1)

    def bias_rows(split, whole):
        query_sum, value_sum, expand_sum = [place_split(part, lay) for part in split]
        output_sum, reduce_sum = whole
        return (
            by_chip(jnp.concatenate([query_sum, value_sum])),
            by_chip(expand_sum),
            by_chip(output_sum),
            by_chip(reduce_sum),
        )

    spatial_rows = bias_rows(spatial_split, spatial_whole)
    temporal_rows = bias_rows(temporal_split, temporal_whole)
    rows = (
        by_chip(table_part.reshape(-1, width)),
        spatial_rows[0],
        spatial_rows[1],
        temporal_rows[0],
        temporal_rows[1],
        by_chip(grad_mod),
        spatial_rows[2],
        spatial_rows[3],
        temporal_rows[2],
        temporal_rows[3],
    )
    summed = cube_scatter(jnp.concatenate(rows, axis=1), "sp", chips)
    sums = split_columns(summed, [row.shape[1] for row in rows])

    mod_low = sums[5].reshape(clips, -1).astype(BF16)
    modulate_bias_grad = jnp.sum(mod_low.astype(F32), axis=0)
    modulate_grad = contract_first(condition_act, mod_low)
    condition_part = project_rows(mod_low, modulate)

    table_sum = sums[0].reshape(clips_here, -1)
    table_pick = (lax.iota(jnp.int32, row_table.shape[0])[:, None] == table_index[None, :]).astype(
        F32
    )
    table_placed = jnp.sum(table_pick[:, :, None] * table_sum[None], axis=1)
    exchanged = jnp.concatenate([table_placed.reshape(-1)] + [sums[k] for k in (1, 2, 3, 4)])
    exchanged = cube_sum(exchanged, "dp", cores)
    tables, s_input_bias, s_expand_bias, t_input_bias, t_expand_bias = split_columns(
        exchanged, [table_placed.size] + [sums[k].shape[0] for k in (1, 2, 3, 4)]
    )
    tables = tables.reshape(row_table.shape[0], 2, 2 * SIDE, -1)

    grad_condition_act = cube_sum(condition_part, "sp", chips)
    silu_back = jax.vjp(jax.nn.silu, condition)[1]
    grad_condition = silu_back(grad_condition_act)[0]
    class_grad = contract_first(class_pick.astype(F32), grad_condition, HIGHEST)
    grad_time = grad_condition.astype(BF16)
    time_second_bias_grad = jnp.sum(grad_time.astype(F32), axis=0)
    time_second_grad = contract_first(time_act, grad_time)
    grad_time_act = project_rows(grad_time, time_second)
    time_silu_back = jax.vjp(jax.nn.silu, time_hidden)[1]
    grad_time_hidden = time_silu_back(grad_time_act)[0].astype(BF16)
    time_first_bias_grad = jnp.sum(grad_time_hidden.astype(F32), axis=0)
    time_first_grad = contract_first(embedding, grad_time_hidden)

    s_input, s_output, s_expand, s_reduce = join_columns(spatial_sums, lay)
    t_input, t_output, t_expand, t_reduce = join_columns(temporal_sums, lay)
    return (
        activations,
        input_grad,
        tables[:, 0],
        tables[:, 1],
        class_grad,
        time_first_grad,
        time_first_bias_grad,
        time_second_grad,
        time_second_bias_grad,
        modulate_grad,
        modulate_bias_grad,
        s_input,
        s_input_bias,
        s_output,
        sums[6],
        s_expand,
        s_expand_bias,
        s_reduce,
        sums[7],
        t_input,
        t_input_bias,
        t_output,
        sums[8],
        t_expand,
        t_expand_bias,
        t_reduce,
        sums[9],
    )


def solution(mesh):
    in_specs = (
        P(("dp", "sp"), None, None),
        P(("dp", "sp"), None, None),
        P("dp"),
        P("dp"),
        P("dp"),
        P("dp"),
        P(),
        P(),
        P(),
        P(),
        P(),
        P(),
        P(),
        P(None, "sp"),
        P("sp"),
        P("sp", None),
        P("sp"),
        P("sp", None),
        P("sp"),
        P("sp", None),
        P("sp"),
        P("sp", None),
        P("sp"),
        P("sp", None),
        P("sp"),
        P("sp", None),
        P("sp"),
        P("sp", None),
        P("sp"),
        P("sp", None),
        P("sp"),
    )
    out_specs = (
        P(("dp", "sp"), None, None),
        P(("dp", "sp"), None, None),
        P(None, None, "sp"),
        P(None, None, "sp"),
        P(),
        P(),
        P(),
        P(),
        P(),
        P(None, "sp"),
        P("sp"),
        P("sp", None),
        P("sp"),
        P("sp", None),
        P("sp"),
        P("sp", None),
        P("sp"),
        P("sp", None),
        P("sp"),
        P("sp", None),
        P("sp"),
        P("sp", None),
        P("sp"),
        P("sp", None),
        P("sp"),
        P("sp", None),
        P("sp"),
    )
    return jax.shard_map(
        partial(per_device, Layout(mesh)), mesh=mesh, in_specs=in_specs, out_specs=out_specs, check_vma=False
    )
```

```python
from functools import partial
import math

import jax
import jax.numpy as jnp
from jax import lax
from jax.experimental import pallas as pl
from jax.experimental.pallas import tpu as pltpu
from jax.sharding import PartitionSpec as P

HEADS = 16
HDIM = 72
FREQ = 256
SIDE = 16
FRAMES = 16

EPSILON = 1e-06
HIGHEST = lax.Precision.HIGHEST
BF16 = jnp.bfloat16
F32 = jnp.float32


def layer_norm(values):
    center = values - jnp.mean(values, axis=-1, keepdims=True)
    inverse = lax.rsqrt(jnp.mean(center * center, axis=-1, keepdims=True) + EPSILON)
    return (center * inverse, inverse)


def norm_back(gradient, normed, inverse):
    mean_grad = jnp.mean(gradient, axis=-1, keepdims=True)
    mean_cross = jnp.mean(gradient * normed, axis=-1, keepdims=True)
    return inverse * (gradient - mean_grad - normed * mean_cross)


def project(left_rows, weight):
    return lax.dot_general(
        left_rows,
        weight,
        (((left_rows.ndim - 1,), (0,)), ((), ())),
        preferred_element_type=F32,
    )


def project_rows(left_rows, weight):
    return lax.dot_general(
        left_rows,
        weight,
        (((left_rows.ndim - 1,), (1,)), ((), ())),
        preferred_element_type=F32,
    )


def contract_first(left_rows, right_rows, precision=None):
    return lax.dot_general(
        left_rows,
        right_rows,
        (((0,), (0,)), ((), ())),
        preferred_element_type=F32,
        precision=precision,
    )


def flat(values):
    return values.reshape(-1, values.shape[-1])


def token_sum(values):
    return jnp.sum(flat(values).astype(F32), axis=0)


def flip(values, axis, size, bit):
    return lax.ppermute(values, axis, [(i, i ^ bit) for i in range(size)])


def bits_of(size):
    bits = []
    bit = 1
    while bit < size:
        bits.append(bit)
        bit = bit * 2
    assert bit == size
    return bits


def cube_gather(values, axis, size):
    rank = lax.axis_index(axis)
    held = values[None]
    for bit in bits_of(size):
        other = flip(held, axis, size, bit)
        upper = (rank & bit) != 0
        held = jnp.concatenate(
            [jnp.where(upper, other, held), jnp.where(upper, held, other)], axis=0
        )
    return held


def cube_sum(values, axis, size):
    for bit in bits_of(size):
        values = values + flip(values, axis, size, bit)
    return values


def cube_scatter(values, axis, size):
    rank = lax.axis_index(axis)
    for bit in reversed(bits_of(size)):
        upper = (rank & bit) != 0
        low, high = values[:bit], values[bit:]
        away = jnp.where(upper, low, high)
        kept = jnp.where(upper, high, low)
        values = kept + flip(away, axis, size, bit)
    return values[0]


def tie(values, others):
    values = list(values)
    return lax.optimization_barrier(tuple(values) + tuple(others))[: len(values)]


def pick(values, axis, index):
    return lax.dynamic_index_in_dim(values, index, axis, keepdims=False)


def add_low(left, right):
    return (left.astype(F32) + right.astype(F32)).astype(BF16)


def hop(values, lay, bit):
    return flip(values, "sp", lay.chips, bit)


def turn(values, lay, offset):
    count = lay.chips
    return lax.ppermute(values, "sp", [(i, (i + 4 * offset) % count) for i in range(count)])


def put_kernel(depth, cut, held_ref, x_ref, y_ref, low_ref, high_ref, out_ref):
    chip = lax.axis_index("sp")
    z, y, x = chip // 4, lax.rem(chip // 2, 2), lax.rem(chip, 2)
    for k in range(depth):
        layer = lax.rem(z + depth - k, depth)
        out_ref[layer, y, x] = held_ref[k]
        out_ref[layer, y, 1 - x] = x_ref[k]
        out_ref[layer, 1 - y, x] = y_ref[k]
        out_ref[layer, 1 - y, 1 - x, :, :cut] = low_ref[k]
        out_ref[layer, 1 - y, 1 - x, :, cut:] = high_ref[k]


def put_rows(arrays, cut):
    depth, rows, columns = arrays[0].shape
    whole = pl.pallas_call(
        partial(put_kernel, depth, cut),
        out_shape=jax.ShapeDtypeStruct((depth, 2, 2, rows, columns), BF16),
        in_specs=[pl.BlockSpec(memory_space=pltpu.VMEM)] * 5,
        out_specs=pl.BlockSpec(memory_space=pltpu.VMEM),
        compiler_params=pltpu.CompilerParams(vmem_limit_bytes=24 << 20),
        cost_estimate=pl.CostEstimate(
            flops=0, transcendentals=0, bytes_accessed=16 * depth * rows * columns
        ),
        name="put_rows",
    )(*arrays)
    return whole.reshape(depth * 4 * rows, columns)


def cut_of(columns):
    return columns // 256 * 128


class Gather:
    def __init__(self, lay):
        self.lay = lay
        self.layers = []
        self.sides = []
        self.corners = []

    def chunk(self, shard):
        lay = self.lay
        cut = cut_of(shard.shape[1])
        after = (self.layers[-1] if self.layers else []) + (
            self.corners[-2] if len(self.corners) > 1 else []
        )
        if after:
            (shard,) = tie([shard], after)
        layers = [turn(shard, lay, k) for k in range(1, lay.chips // 4)]
        held = jnp.stack([shard] + layers)
        if self.sides:
            (held,) = tie([held], self.sides[-1])
        along_x, along_y = hop(held, lay, 1), hop(held, lay, 2)
        low = hop(along_x[:, :, :cut], lay, 2)
        high = hop(along_y[:, :, cut:], lay, 1)
        self.layers.append(layers)
        self.sides.append([along_x, along_y])
        self.corners.append([low, high])
        return put_rows([held, along_x, along_y, low, high], cut)


class Scatter:
    def __init__(self, lay):
        self.lay = lay
        self.layers = []
        self.sides = []
        self.corners = []

    def chunk(self, grad):
        lay = self.lay
        depth = lay.chips // 4
        chip = lax.axis_index("sp")
        z, y, x = chip // 4, (chip // 2) % 2, chip % 2
        cut = cut_of(grad.shape[1])
        grid = grad.reshape(depth, 2, 2, -1, grad.shape[1])

        def at(row, column):
            return pick(pick(grid, 1, row), 1, column)

        corner = at(1 - y, 1 - x)
        low, high = corner[..., :cut], corner[..., cut:]
        after = (self.corners[-1] if self.corners else []) + (
            self.sides[-2] if len(self.sides) > 1 else []
        )
        if after:
            low, high = tie([low, high], after)
        low_got, high_got = hop(low, lay, 2), hop(high, lay, 1)
        side_x, side_y = at(y, 1 - x), at(1 - y, x)
        send_x = jnp.concatenate([add_low(side_x[..., :cut], low_got), side_x[..., cut:]], axis=-1)
        send_y = jnp.concatenate([side_y[..., :cut], add_low(side_y[..., cut:], high_got)], axis=-1)
        if len(self.layers) > 1:
            send_x, send_y = tie([send_x, send_y], self.layers[-2])
        got_x, got_y = hop(send_x, lay, 1), hop(send_y, lay, 2)
        own = at(y, x)

        def part(layer):
            return (
                pick(own, 0, layer).astype(F32)
                + pick(got_x, 0, layer).astype(F32)
                + pick(got_y, 0, layer).astype(F32)
            )

        layers = [turn(part((z + k) % depth).astype(BF16), lay, k) for k in range(1, depth)]
        total = part(z)
        for got in layers:
            total = total + got.astype(F32)
        self.layers.append(layers)
        self.sides.append([got_x, got_y])
        self.corners.append([low_got, high_got])
        return total


def attention_scores(query, key, stride):
    scores = jnp.einsum("snhd,smhd->shnm", query, key, preferred_element_type=F32)
    scores = scores * HDIM ** (-0.5)
    if stride > 1:
        count = scores.shape[-1]
        row = lax.broadcasted_iota(jnp.int32, (count, count), 0) % stride
        col = lax.broadcasted_iota(jnp.int32, (count, count), 1) % stride
        scores = jnp.where(row == col, scores, -1e30)
    return scores


def attend(query, key, value, stride):
    scores = attention_scores(query, key, stride)
    row_max = jnp.max(scores, axis=-1, keepdims=True)
    exponent = jnp.exp(scores - row_max)
    row_total = jnp.sum(exponent, axis=-1, keepdims=True)
    probs = (exponent / row_total).astype(BF16)
    mixed = jnp.einsum("shnm,smhd->snhd", probs, value, preferred_element_type=F32)
    return (mixed.astype(BF16), row_max + jnp.log(row_total))


def attend_back(query, key, value, logsum, grad_out, stride):
    scale = HDIM ** (-0.5)
    probs = jnp.exp(attention_scores(query, key, stride) - logsum)
    grad_probs = jnp.einsum("snhd,smhd->shnm", grad_out, value, preferred_element_type=F32)
    inner = jnp.sum(probs * grad_probs, axis=-1, keepdims=True)
    grad_scores = (probs * (grad_probs - inner)).astype(BF16)
    grad_query = (
        jnp.einsum("shnm,smhd->snhd", grad_scores, key, preferred_element_type=F32) * scale
    )
    grad_key = (
        jnp.einsum("shnm,snhd->smhd", grad_scores, query, preferred_element_type=F32) * scale
    )
    grad_value = jnp.einsum(
        "shnm,snhd->smhd", probs.astype(BF16), grad_out, preferred_element_type=F32
    )
    return (grad_query.astype(BF16), grad_key.astype(BF16), grad_value.astype(BF16))


class Layout:
    def __init__(self, mesh):
        self.cores = mesh.shape["dp"]
        self.chips = mesh.shape["sp"]
        self.heads = HEADS // self.cores


def core_total(values, lay):
    total = values.astype(BF16).astype(F32)
    for bit in bits_of(lay.cores):
        total = total + flip(total.astype(BF16), "dp", lay.cores, bit).astype(F32)
    return total


def core_part(values, axis, lay):
    share = values.shape[axis] // lay.cores
    return lax.dynamic_slice_in_dim(values, lax.axis_index("dp") * share, share, axis)


def heads_of(values, sequences, lay):
    return values.reshape(sequences, -1, lay.heads, HDIM)


def block_forward(inputs, modulation, weights, biases, stride, lay):
    w_input, w_output, w_expand, w_reduce = weights
    query_bias, value_bias, output_bias, expand_bias, reduce_bias = biases
    groups, count, width = inputs.shape
    share = width // lay.cores
    shift_att, scale_att, gate_att, shift_mlp, scale_mlp, gate_mlp = jnp.split(
        modulation[:, None, :], 6, axis=-1
    )
    normed_att, inverse_att = layer_norm(inputs)
    attn_input = (normed_att * (1.0 + scale_att) + shift_att).astype(BF16)
    projected = project(attn_input, w_input)
    query = heads_of((projected[..., :share] + query_bias).astype(BF16), groups, lay)
    key = heads_of(projected[..., share : 2 * share].astype(BF16), groups, lay)
    value = heads_of((projected[..., 2 * share :] + value_bias).astype(BF16), groups, lay)
    mixed, logsum = attend(query, key, value, stride)
    attended = mixed.reshape(groups, count, share)
    branch = core_total(project_rows(attended, w_output), lay) + output_bias
    hidden = inputs + gate_att * branch
    normed_mlp, inverse_mlp = layer_norm(hidden)
    mlp_input = (normed_mlp * (1.0 + scale_mlp) + shift_mlp).astype(BF16)
    expanded = project(mlp_input, w_expand) + expand_bias
    activated = jax.nn.gelu(expanded, approximate=True).astype(BF16)
    reduced = core_total(project_rows(activated, w_reduce), lay) + reduce_bias
    output = hidden + gate_mlp * reduced
    kept = (
        normed_att,
        inverse_att,
        attn_input,
        query,
        key,
        value,
        attended,
        logsum,
        branch,
        normed_mlp,
        inverse_mlp,
        mlp_input,
        expanded,
        activated,
        reduced,
    )
    return (output, kept)


def block_backward(gradient, kept, modulation, weights, stride, lay):
    w_input, w_output, w_expand, w_reduce = weights
    (
        normed_att,
        inverse_att,
        attn_input,
        query,
        key,
        value,
        attended,
        logsum,
        branch,
        normed_mlp,
        inverse_mlp,
        mlp_input,
        expanded,
        activated,
        reduced,
    ) = kept
    groups, count, width = gradient.shape
    share = width // lay.cores
    shift_att, scale_att, gate_att, shift_mlp, scale_mlp, gate_mlp = jnp.split(
        modulation[:, None, :], 6, axis=-1
    )
    grad_gate_mlp = jnp.sum(gradient * reduced, axis=1)
    grad_reduced = (gradient * gate_mlp).astype(BF16)
    reduce_grad = contract_first(flat(grad_reduced), flat(activated)).astype(BF16)
    grad_activated = project(grad_reduced, w_reduce)
    gelu_back = jax.vjp(partial(jax.nn.gelu, approximate=True), expanded)[1]
    grad_expanded = gelu_back(grad_activated)[0].astype(BF16)
    expand_grad = contract_first(flat(mlp_input), flat(grad_expanded)).astype(BF16)
    grad_mlp_input = core_total(project_rows(grad_expanded, w_expand), lay)
    grad_scale_mlp = jnp.sum(grad_mlp_input * normed_mlp, axis=1)
    grad_shift_mlp = jnp.sum(grad_mlp_input, axis=1)
    grad_hidden = gradient + norm_back(grad_mlp_input * (1.0 + scale_mlp), normed_mlp, inverse_mlp)
    grad_gate_att = jnp.sum(grad_hidden * branch, axis=1)
    grad_branch = (grad_hidden * gate_att).astype(BF16)
    grad_attended = project(grad_branch, w_output).astype(BF16)
    grad_query, grad_key, grad_value = attend_back(
        query, key, value, logsum, heads_of(grad_attended, groups, lay), stride
    )
    grad_query = grad_query.reshape(groups, count, share)
    grad_key = grad_key.reshape(groups, count, share)
    grad_value = grad_value.reshape(groups, count, share)
    grad_projected = jnp.concatenate([grad_query, grad_key, grad_value], axis=-1)
    left = jnp.concatenate([flat(attn_input), flat(grad_branch)], axis=0)
    right = jnp.concatenate(
        [
            jnp.pad(flat(grad_projected), ((0, 0), (0, share))),
            jnp.pad(flat(attended), ((0, 0), (3 * share, 0))),
        ],
        axis=0,
    )
    attention_grad = contract_first(left, right).astype(BF16)
    grad_attn_input = core_total(project_rows(grad_projected, w_input), lay)
    grad_scale_att = jnp.sum(grad_attn_input * normed_att, axis=1)
    grad_shift_att = jnp.sum(grad_attn_input, axis=1)
    grad_inputs = grad_hidden + norm_back(
        grad_attn_input * (1.0 + scale_att), normed_att, inverse_att
    )
    grad_mod = jnp.concatenate(
        [
            grad_shift_att,
            grad_scale_att,
            grad_gate_att,
            grad_shift_mlp,
            grad_scale_mlp,
            grad_gate_mlp,
        ],
        axis=-1,
    )
    split_biases = (token_sum(grad_query), token_sum(grad_value), token_sum(grad_expanded))
    whole_biases = (token_sum(grad_branch), token_sum(grad_reduced))
    return (
        grad_inputs,
        grad_mod,
        split_biases,
        whole_biases,
        (attention_grad, expand_grad, reduce_grad),
    )


def shard_parts(w_input, w_output, w_expand, w_reduce, lay):
    rows = w_input.shape[0]
    attention = core_part(w_input.reshape(rows, 3, -1), 2, lay).reshape(rows, -1)
    return (
        attention,
        core_part(w_output, 1, lay),
        core_part(w_expand, 1, lay),
        core_part(w_reduce, 1, lay),
    )


def split_columns(values, widths):
    bounds = []
    offset = 0
    for width in widths[:-1]:
        offset = offset + width
        bounds.append(offset)
    return jnp.split(values, bounds, axis=-1)


def fetch_weights(gather, w_input, w_output, w_expand, w_reduce, lay):
    c_input, c_output, c_expand, c_reduce = shard_parts(w_input, w_output, w_expand, w_reduce, lay)
    attention = gather.chunk(jnp.concatenate([c_input, c_output], axis=1))
    expand = gather.chunk(c_expand)
    reduce = gather.chunk(c_reduce)
    count = c_input.shape[1]
    return (attention[:, :count], attention[:, count:], expand, reduce)


def fetch_whole(w_input, w_output, w_expand, w_reduce, lay):
    parts = shard_parts(w_input, w_output, w_expand, w_reduce, lay)
    whole = lax.all_gather(jnp.concatenate(parts, axis=1), "sp", axis=0, tiled=True)
    return split_columns(whole, [part.shape[1] for part in parts])


def sum_chips(grad):
    return lax.psum_scatter(grad, "sp", scatter_dimension=0, tiled=True)


def reduce_whole(grads):
    g_attention, g_expand, g_reduce = grads
    attention = sum_chips(g_attention)
    count = g_attention.shape[1] * 3 // 4
    return (attention[:, :count], attention[:, count:], sum_chips(g_expand), sum_chips(g_reduce))


def reduce_weights(scatter, grads):
    g_attention, g_expand, g_reduce = grads
    reduce = scatter.chunk(g_reduce)
    expand = scatter.chunk(g_expand)
    attention = scatter.chunk(g_attention)
    count = g_attention.shape[1] * 3 // 4
    return (attention[:, :count], attention[:, count:], expand, reduce)


def join_columns(parts, lay):
    g_input, g_output, g_expand, g_reduce = [
        cube_gather(part.astype(BF16), "dp", lay.cores).astype(F32) for part in parts
    ]
    rows = g_output.shape[1]
    thirds = g_input.reshape(lay.cores, rows, 3, -1)
    return (
        jnp.transpose(thirds, (1, 2, 0, 3)).reshape(rows, -1),
        jnp.transpose(g_output, (1, 0, 2)).reshape(rows, -1),
        jnp.transpose(g_expand, (1, 0, 2)).reshape(rows, -1),
        jnp.transpose(g_reduce, (1, 0, 2)).reshape(rows, -1),
    )


def to_positions(values, clips, lay):
    moved = lax.all_to_all(values, "sp", split_axis=1, concat_axis=0, tiled=True)
    moved = moved.reshape(clips, -1, values.shape[-1])
    return cube_gather(moved, "dp", lay.cores).reshape(-1, moved.shape[1], moved.shape[2])


def own_group(values, lay):
    share = values.shape[0] // lay.cores
    return lax.dynamic_slice_in_dim(values, lax.axis_index("dp") * share, share, 0)


def to_frames(values, frames_here, lay):
    own = own_group(values, lay)
    own = own.reshape(frames_here * lay.chips, -1, values.shape[-1])
    return lax.all_to_all(own, "sp", split_axis=0, concat_axis=1, tiled=True)


def place_split(values, lay):
    whole = jnp.zeros((lay.cores,) + values.shape, values.dtype)
    whole = lax.dynamic_update_index_in_dim(whole, values, lax.axis_index("dp"), 0)
    return whole.reshape(-1)


def per_device(
    lay,
    frames,
    cotangent,
    aspect,
    table_index,
    noise_level,
    labels,
    row_table,
    column_table,
    class_table,
    time_first,
    time_first_bias,
    time_second,
    time_second_bias,
    modulate,
    modulate_bias,
    spatial_input,
    spatial_input_bias,
    spatial_output,
    spatial_output_bias,
    spatial_expand,
    spatial_expand_bias,
    spatial_reduce,
    spatial_reduce_bias,
    temporal_input,
    temporal_input_bias,
    temporal_output,
    temporal_output_bias,
    temporal_expand,
    temporal_expand_bias,
    temporal_reduce,
    temporal_reduce_bias,
):
    cores, chips = lay.cores, lay.chips
    chip = lax.axis_index("sp")
    core = lax.axis_index("dp")
    frame_count, patches, width = frames.shape
    clips_here = aspect.shape[0]
    clips = cores * clips_here
    clip_here = chip * frame_count // FRAMES

    gather = Gather(lay)
    scatter = Scatter(lay)
    spatial_weights = fetch_weights(
        gather, spatial_input, spatial_output, spatial_expand, spatial_reduce, lay
    )
    temporal_weights = fetch_whole(
        temporal_input, temporal_output, temporal_expand, temporal_reduce, lay
    )

    facts = cube_gather(jnp.stack([aspect, table_index, noise_level, labels]), "dp", cores)
    group_aspect, group_table = (
        lax.dynamic_index_in_dim(facts[:, k], clip_here, 1, keepdims=False) for k in (0, 1)
    )
    all_levels = facts[:, 2].reshape(clips)
    all_labels = facts[:, 3].reshape(clips)
    group_clips = jnp.arange(cores) * clips_here + clip_here

    half = FREQ // 2
    frequency = jnp.exp(-math.log(10000.0) * jnp.arange(half, dtype=F32) / half)
    angles = all_levels.astype(F32)[:, None] * frequency[None, :]
    embedding = jnp.concatenate([jnp.cos(angles), jnp.sin(angles)], axis=-1).astype(BF16)
    time_hidden = project(embedding, time_first) + time_first_bias.astype(F32)
    time_act = jax.nn.silu(time_hidden).astype(BF16)
    class_pick = (all_labels[:, None] == lax.iota(jnp.int32, class_table.shape[0])[None, :]).astype(
        BF16
    )
    condition = (
        project(time_act, time_second)
        + time_second_bias.astype(F32)
        + project(class_pick, class_table)
    )
    condition_act = jax.nn.silu(condition).astype(BF16)
    mod_cols = project(condition_act, modulate) + modulate_bias.astype(F32)

    bias_shards = (
        spatial_input_bias,
        spatial_output_bias,
        spatial_expand_bias,
        spatial_reduce_bias,
        temporal_input_bias,
        temporal_output_bias,
        temporal_expand_bias,
        temporal_reduce_bias,
    )
    bias_sizes = [shard.shape[0] for shard in bias_shards]
    small = jnp.concatenate([mod_cols.reshape(-1)] + [shard.astype(F32) for shard in bias_shards])
    gathered = cube_gather(small, "sp", chips)
    mod_size = mod_cols.shape[1]
    pieces = split_columns(gathered, [clips * mod_size] + bias_sizes)
    modulation = jnp.transpose(pieces[0].reshape(chips, clips, mod_size), (1, 0, 2)).reshape(
        clips, chips * mod_size
    )
    whole_biases = [piece.reshape(-1) for piece in pieces[1:]]

    def block_biases(parts):
        query_bias, value_bias = jnp.split(parts[0], 2)
        return (
            core_part(query_bias, 0, lay),
            core_part(value_bias, 0, lay),
            parts[1],
            core_part(parts[2], 0, lay),
            parts[3],
        )

    spatial_biases = block_biases(whole_biases[:4])
    temporal_biases = block_biases(whole_biases[4:])
    clip_pick = (group_clips[:, None] == jnp.arange(clips)[None, :]).astype(F32)
    spatial_mod = jnp.sum(
        clip_pick[:, :, None] * modulation[None, :, : 6 * width], axis=1
    )
    temporal_mod = modulation[:, 6 * width :]

    row_width = jnp.where(
        group_aspect == 0, SIDE, jnp.where(group_aspect == 1, 2 * SIDE, SIDE // 2)
    )[:, None, None]
    patch_ids = lax.iota(jnp.int32, patches)[None, :, None]
    grid_ids = lax.iota(jnp.int32, 2 * SIDE)[None, None, :]
    row_pick = (patch_ids // row_width == grid_ids).astype(BF16)
    col_pick = (patch_ids % row_width == grid_ids).astype(BF16)
    row_chosen = jnp.take(row_table, group_table, axis=0)
    col_chosen = jnp.take(column_table, group_table, axis=0)
    positions = jnp.einsum(
        "gpr,grd->gpd", row_pick, row_chosen, preferred_element_type=F32
    ) + jnp.einsum("gpr,grd->gpd", col_pick, col_chosen, preferred_element_type=F32)
    all_frames = cube_gather(frames, "dp", cores).astype(F32)
    block_input = (all_frames + positions[:, None]).reshape(-1, patches, width)
    frame_mod = jnp.repeat(spatial_mod, frame_count, axis=0)

    spatial_out, spatial_kept = block_forward(
        block_input, frame_mod, spatial_weights, spatial_biases, 1, lay
    )
    own_out = own_group(spatial_out.astype(BF16), lay)
    between = to_positions(own_out, clips_here, lay)
    local_patches = patches // chips
    temporal_out, temporal_kept = block_forward(
        between.astype(F32), temporal_mod, temporal_weights, temporal_biases, local_patches, lay
    )
    activations = to_frames(temporal_out.astype(BF16), frame_count, lay)
    grad_after = to_positions(cotangent, clips_here, lay)
    grad_between, temporal_dmod, temporal_split, temporal_whole, temporal_grads = block_backward(
        grad_after.astype(F32), temporal_kept, temporal_mod, temporal_weights, local_patches, lay
    )
    temporal_sums = reduce_whole(temporal_grads)
    own_grad = to_frames(grad_between.astype(BF16), frame_count, lay)
    grad_frames = cube_gather(own_grad, "dp", cores).reshape(-1, patches, width)
    input_grad_all, frame_dmod, spatial_split, spatial_whole, spatial_grads = block_backward(
        grad_frames.astype(F32), spatial_kept, frame_mod, spatial_weights, 1, lay
    )
    spatial_sums = reduce_weights(scatter, spatial_grads)
    input_grad = own_group(input_grad_all, lay)

    grad_positions = jnp.sum(input_grad, axis=0)
    own_rows = lax.dynamic_index_in_dim(row_pick, core, 0, keepdims=False).astype(F32)
    own_cols = lax.dynamic_index_in_dim(col_pick, core, 0, keepdims=False).astype(F32)
    table_part = contract_first(
        jnp.concatenate([own_rows, own_cols], axis=1), grad_positions, HIGHEST
    )
    here = (lax.iota(jnp.int32, clips_here) == clip_here).astype(F32)
    table_part = here[:, None, None] * table_part[None]

    spatial_dmod = jnp.sum(frame_dmod.reshape(cores, frame_count, -1), axis=1)
    spatial_dmod = jnp.sum(clip_pick[:, :, None] * spatial_dmod[:, None, :], axis=0)
    grad_mod = jnp.concatenate([spatial_dmod, temporal_dmod], axis=-1)

    def by_chip(values):
        parts = values.reshape(-1, chips, values.shape[-1] // chips)
        return jnp.transpose(parts, (1, 0, 2)).reshape(chips, -1)

    def bias_rows(split, whole):
        query_sum, value_sum, expand_sum = [place_split(part, lay) for part in split]
        output_sum, reduce_sum = whole
        return (
            by_chip(jnp.concatenate([query_sum, value_sum])),
            by_chip(expand_sum),
            by_chip(output_sum),
            by_chip(reduce_sum),
        )

    spatial_rows = bias_rows(spatial_split, spatial_whole)
    temporal_rows = bias_rows(temporal_split, temporal_whole)
    rows = (
        by_chip(table_part.reshape(-1, width)),
        spatial_rows[0],
        spatial_rows[1],
        temporal_rows[0],
        temporal_rows[1],
        by_chip(grad_mod),
        spatial_rows[2],
        spatial_rows[3],
        temporal_rows[2],
        temporal_rows[3],
    )
    summed = cube_scatter(jnp.concatenate(rows, axis=1), "sp", chips)
    sums = split_columns(summed, [row.shape[1] for row in rows])

    mod_low = sums[5].reshape(clips, -1).astype(BF16)
    modulate_bias_grad = jnp.sum(mod_low.astype(F32), axis=0)
    modulate_grad = contract_first(condition_act, mod_low)
    condition_part = project_rows(mod_low, modulate)

    table_sum = sums[0].reshape(clips_here, -1)
    table_pick = (lax.iota(jnp.int32, row_table.shape[0])[:, None] == table_index[None, :]).astype(
        F32
    )
    table_placed = jnp.sum(table_pick[:, :, None] * table_sum[None], axis=1)
    exchanged = jnp.concatenate([table_placed.reshape(-1)] + [sums[k] for k in (1, 2, 3, 4)])
    exchanged = cube_sum(exchanged, "dp", cores)
    tables, s_input_bias, s_expand_bias, t_input_bias, t_expand_bias = split_columns(
        exchanged, [table_placed.size] + [sums[k].shape[0] for k in (1, 2, 3, 4)]
    )
    tables = tables.reshape(row_table.shape[0], 2, 2 * SIDE, -1)

    grad_condition_act = cube_sum(condition_part, "sp", chips)
    silu_back = jax.vjp(jax.nn.silu, condition)[1]
    grad_condition = silu_back(grad_condition_act)[0]
    class_grad = contract_first(class_pick.astype(F32), grad_condition, HIGHEST)
    grad_time = grad_condition.astype(BF16)
    time_second_bias_grad = jnp.sum(grad_time.astype(F32), axis=0)
    time_second_grad = contract_first(time_act, grad_time)
    grad_time_act = project_rows(grad_time, time_second)
    time_silu_back = jax.vjp(jax.nn.silu, time_hidden)[1]
    grad_time_hidden = time_silu_back(grad_time_act)[0].astype(BF16)
    time_first_bias_grad = jnp.sum(grad_time_hidden.astype(F32), axis=0)
    time_first_grad = contract_first(embedding, grad_time_hidden)

    s_input, s_output, s_expand, s_reduce = join_columns(spatial_sums, lay)
    t_input, t_output, t_expand, t_reduce = join_columns(temporal_sums, lay)
    return (
        activations,
        input_grad,
        tables[:, 0],
        tables[:, 1],
        class_grad,
        time_first_grad,
        time_first_bias_grad,
        time_second_grad,
        time_second_bias_grad,
        modulate_grad,
        modulate_bias_grad,
        s_input,
        s_input_bias,
        s_output,
        sums[6],
        s_expand,
        s_expand_bias,
        s_reduce,
        sums[7],
        t_input,
        t_input_bias,
        t_output,
        sums[8],
        t_expand,
        t_expand_bias,
        t_reduce,
        sums[9],
    )


def solution(mesh):
    in_specs = (
        P(("dp", "sp"), None, None),
        P(("dp", "sp"), None, None),
        P("dp"),
        P("dp"),
        P("dp"),
        P("dp"),
        P(),
        P(),
        P(),
        P(),
        P(),
        P(),
        P(),
        P(None, "sp"),
        P("sp"),
        P("sp", None),
        P("sp"),
        P("sp", None),
        P("sp"),
        P("sp", None),
        P("sp"),
        P("sp", None),
        P("sp"),
        P("sp", None),
        P("sp"),
        P("sp", None),
        P("sp"),
        P("sp", None),
        P("sp"),
        P("sp", None),
        P("sp"),
    )
    out_specs = (
        P(("dp", "sp"), None, None),
        P(("dp", "sp"), None, None),
        P(None, None, "sp"),
        P(None, None, "sp"),
        P(),
        P(),
        P(),
        P(),
        P(),
        P(None, "sp"),
        P("sp"),
        P("sp", None),
        P("sp"),
        P("sp", None),
        P("sp"),
        P("sp", None),
        P("sp"),
        P("sp", None),
        P("sp"),
        P("sp", None),
        P("sp"),
        P("sp", None),
        P("sp"),
        P("sp", None),
        P("sp"),
        P("sp", None),
        P("sp"),
    )
    return jax.shard_map(
        partial(per_device, Layout(mesh)), mesh=mesh, in_specs=in_specs, out_specs=out_specs, check_vma=False
    )
```

```python
from functools import partial
import math

import jax
import jax.numpy as jnp
from jax import lax
from jax.experimental import pallas as pl
from jax.experimental.pallas import tpu as pltpu
from jax.sharding import PartitionSpec as P

HEADS = 16
HDIM = 72
FREQ = 256
SIDE = 16
FRAMES = 16

EPSILON = 1e-06
HIGHEST = lax.Precision.HIGHEST
BF16 = jnp.bfloat16
F32 = jnp.float32


def layer_norm(values):
    center = values - jnp.mean(values, axis=-1, keepdims=True)
    inverse = lax.rsqrt(jnp.mean(center * center, axis=-1, keepdims=True) + EPSILON)
    return (center * inverse, inverse)


def norm_back(gradient, normed, inverse):
    mean_grad = jnp.mean(gradient, axis=-1, keepdims=True)
    mean_cross = jnp.mean(gradient * normed, axis=-1, keepdims=True)
    return inverse * (gradient - mean_grad - normed * mean_cross)


def project(left_rows, weight):
    return lax.dot_general(
        left_rows,
        weight,
        (((left_rows.ndim - 1,), (0,)), ((), ())),
        preferred_element_type=F32,
    )


def project_rows(left_rows, weight):
    return lax.dot_general(
        left_rows,
        weight,
        (((left_rows.ndim - 1,), (1,)), ((), ())),
        preferred_element_type=F32,
    )


def contract_first(left_rows, right_rows, precision=None):
    return lax.dot_general(
        left_rows,
        right_rows,
        (((0,), (0,)), ((), ())),
        preferred_element_type=F32,
        precision=precision,
    )


def flat(values):
    return values.reshape(-1, values.shape[-1])


def token_sum(values):
    return jnp.sum(flat(values).astype(F32), axis=0)


def flip(values, axis, size, bit):
    return lax.ppermute(values, axis, [(i, i ^ bit) for i in range(size)])


def bits_of(size):
    bits = []
    bit = 1
    while bit < size:
        bits.append(bit)
        bit = bit * 2
    assert bit == size
    return bits


def cube_gather(values, axis, size):
    rank = lax.axis_index(axis)
    held = values[None]
    for bit in bits_of(size):
        other = flip(held, axis, size, bit)
        upper = (rank & bit) != 0
        held = jnp.concatenate(
            [jnp.where(upper, other, held), jnp.where(upper, held, other)], axis=0
        )
    return held


def cube_sum(values, axis, size):
    for bit in bits_of(size):
        values = values + flip(values, axis, size, bit)
    return values


def cube_scatter(values, axis, size):
    rank = lax.axis_index(axis)
    for bit in reversed(bits_of(size)):
        upper = (rank & bit) != 0
        low, high = values[:bit], values[bit:]
        away = jnp.where(upper, low, high)
        kept = jnp.where(upper, high, low)
        values = kept + flip(away, axis, size, bit)
    return values[0]


def tie(values, others):
    values = list(values)
    return lax.optimization_barrier(tuple(values) + tuple(others))[: len(values)]


def pick(values, axis, index):
    return lax.dynamic_index_in_dim(values, index, axis, keepdims=False)


def add_low(left, right):
    return (left.astype(F32) + right.astype(F32)).astype(BF16)


def hop(values, lay, bit):
    return flip(values, "sp", lay.chips, bit)


def turn(values, lay, offset):
    count = lay.chips
    return lax.ppermute(values, "sp", [(i, (i + 4 * offset) % count) for i in range(count)])


def put_kernel(depth, cut, held_ref, x_ref, y_ref, low_ref, high_ref, out_ref):
    chip = lax.axis_index("sp")
    z, y, x = chip // 4, lax.rem(chip // 2, 2), lax.rem(chip, 2)
    for k in range(depth):
        layer = lax.rem(z + depth - k, depth)
        out_ref[layer, y, x] = held_ref[k]
        out_ref[layer, y, 1 - x] = x_ref[k]
        out_ref[layer, 1 - y, x] = y_ref[k]
        out_ref[layer, 1 - y, 1 - x, :, :cut] = low_ref[k]
        out_ref[layer, 1 - y, 1 - x, :, cut:] = high_ref[k]


def put_rows(arrays, cut):
    depth, rows, columns = arrays[0].shape
    whole = pl.pallas_call(
        partial(put_kernel, depth, cut),
        out_shape=jax.ShapeDtypeStruct((depth, 2, 2, rows, columns), BF16),
        in_specs=[pl.BlockSpec(memory_space=pltpu.VMEM)] * 5,
        out_specs=pl.BlockSpec(memory_space=pltpu.VMEM),
        compiler_params=pltpu.CompilerParams(vmem_limit_bytes=24 << 20),
        cost_estimate=pl.CostEstimate(
            flops=0, transcendentals=0, bytes_accessed=16 * depth * rows * columns
        ),
        name="put_rows",
    )(*arrays)
    return whole.reshape(depth * 4 * rows, columns)


def cut_of(columns):
    return columns // 256 * 128


class Gather:
    def __init__(self, lay):
        self.lay = lay
        self.layers = []
        self.sides = []
        self.corners = []

    def chunk(self, shard):
        lay = self.lay
        cut = cut_of(shard.shape[1])
        after = (self.layers[-1] if self.layers else []) + (
            self.corners[-2] if len(self.corners) > 1 else []
        )
        if after:
            (shard,) = tie([shard], after)
        layers = [turn(shard, lay, k) for k in range(1, lay.chips // 4)]
        held = jnp.stack([shard] + layers)
        if self.sides:
            (held,) = tie([held], self.sides[-1])
        along_x, along_y = hop(held, lay, 1), hop(held, lay, 2)
        low = hop(along_x[:, :, :cut], lay, 2)
        high = hop(along_y[:, :, cut:], lay, 1)
        self.layers.append(layers)
        self.sides.append([along_x, along_y])
        self.corners.append([low, high])
        return put_rows([held, along_x, along_y, low, high], cut)


class Scatter:
    def __init__(self, lay):
        self.lay = lay
        self.layers = []
        self.sides = []
        self.corners = []

    def chunk(self, grad, first=(), second=()):
        lay = self.lay
        depth = lay.chips // 4
        chip = lax.axis_index("sp")
        z, y, x = chip // 4, (chip // 2) % 2, chip % 2
        cut = cut_of(grad.shape[1])
        grid = grad.reshape(depth, 2, 2, -1, grad.shape[1])

        def at(row, column):
            return pick(pick(grid, 1, row), 1, column)

        corner = at(1 - y, 1 - x)
        low, high = corner[..., :cut], corner[..., cut:]
        after = (self.corners[-1] if self.corners else []) + (
            self.sides[-2] if len(self.sides) > 1 else []
        )
        if after:
            low, high = tie([low, high], after)
        low_got, high_got = hop(low, lay, 2), hop(high, lay, 1)
        side_x, side_y = at(y, 1 - x), at(1 - y, x)
        send_x = jnp.concatenate([add_low(side_x[..., :cut], low_got), side_x[..., cut:]], axis=-1)
        send_y = jnp.concatenate([side_y[..., :cut], add_low(side_y[..., cut:], high_got)], axis=-1)
        if len(self.layers) > 1:
            send_x, send_y = tie([send_x, send_y], self.layers[-2])
        got_x, got_y = hop(send_x, lay, 1), hop(send_y, lay, 2)
        own = at(y, x)
        got_x, got_y, *first = tie([got_x, got_y] + list(first), [])

        def part(layer):
            return (
                pick(own, 0, layer).astype(F32)
                + pick(got_x, 0, layer).astype(F32)
                + pick(got_y, 0, layer).astype(F32)
            )

        layers = [turn(part((z + k) % depth).astype(BF16), lay, k) for k in range(1, depth)]
        tied = tie(list(layers) + list(second), [])
        layers, second = tied[: depth - 1], tied[depth - 1 :]
        total = part(z)
        for got in layers:
            total = total + got.astype(F32)
        self.layers.append(layers)
        self.sides.append([got_x, got_y])
        self.corners.append([low_got, high_got])
        return (total, list(first), list(second))


def tile_of(columns):
    for tile in (384, 256, 128):
        if columns % tile == 0:
            return tile
    return columns


def fixed_spec(array):
    return pl.BlockSpec(array.shape, lambda j: (0, 0))


def weight_grad(left, right, offset, total, joined=None):
    depth, rows = left.shape
    columns = right.shape[1]
    tile = tile_of(math.gcd(columns, offset) if offset else columns)
    skip = offset // tile

    def body(left_ref, right_ref, *refs):
        out_ref, turned_ref = refs[-2:]

        @pl.when(pl.program_id(0) == 0)
        def _():
            turned_ref[...] = left_ref[...].T

        out_ref[...] = jnp.dot(
            turned_ref[...], right_ref[...], preferred_element_type=F32
        ).astype(BF16)

    held = [] if joined is None else [joined]
    return pl.pallas_call(
        body,
        grid=(columns // tile,),
        in_specs=[fixed_spec(left), pl.BlockSpec((depth, tile), lambda j: (0, j))]
        + [pl.BlockSpec(memory_space=pl.ANY)] * len(held),
        out_specs=pl.BlockSpec((rows, tile), lambda j: (0, j + skip)),
        out_shape=jax.ShapeDtypeStruct((rows, total), BF16),
        scratch_shapes=[pltpu.VMEM((rows, depth), BF16)],
        input_output_aliases={2: 0} if held else {},
        compiler_params=pltpu.CompilerParams(
            dimension_semantics=("arbitrary",), vmem_limit_bytes=40 << 20
        ),
        cost_estimate=pl.CostEstimate(
            flops=2 * depth * rows * columns,
            transcendentals=0,
            bytes_accessed=2 * (depth * rows + depth * columns + rows * columns),
        ),
        name="weight_grad",
    )(left, right, *held)


def attention_scores(query, key, stride):
    scores = jnp.einsum("snhd,smhd->shnm", query, key, preferred_element_type=F32)
    scores = scores * HDIM ** (-0.5)
    if stride > 1:
        count = scores.shape[-1]
        row = lax.broadcasted_iota(jnp.int32, (count, count), 0) % stride
        col = lax.broadcasted_iota(jnp.int32, (count, count), 1) % stride
        scores = jnp.where(row == col, scores, -1e30)
    return scores


def attend(query, key, value, stride):
    scores = attention_scores(query, key, stride)
    row_max = jnp.max(scores, axis=-1, keepdims=True)
    exponent = jnp.exp(scores - row_max)
    row_total = jnp.sum(exponent, axis=-1, keepdims=True)
    probs = (exponent / row_total).astype(BF16)
    mixed = jnp.einsum("shnm,smhd->snhd", probs, value, preferred_element_type=F32)
    return (mixed.astype(BF16), row_max + jnp.log(row_total))


def attend_back(query, key, value, logsum, grad_out, stride):
    scale = HDIM ** (-0.5)
    probs = jnp.exp(attention_scores(query, key, stride) - logsum)
    grad_probs = jnp.einsum("snhd,smhd->shnm", grad_out, value, preferred_element_type=F32)
    inner = jnp.sum(probs * grad_probs, axis=-1, keepdims=True)
    grad_scores = (probs * (grad_probs - inner)).astype(BF16)
    grad_query = (
        jnp.einsum("shnm,smhd->snhd", grad_scores, key, preferred_element_type=F32) * scale
    )
    grad_key = (
        jnp.einsum("shnm,snhd->smhd", grad_scores, query, preferred_element_type=F32) * scale
    )
    grad_value = jnp.einsum(
        "shnm,snhd->smhd", probs.astype(BF16), grad_out, preferred_element_type=F32
    )
    return (grad_query.astype(BF16), grad_key.astype(BF16), grad_value.astype(BF16))


class Layout:
    def __init__(self, mesh):
        self.cores = mesh.shape["dp"]
        self.chips = mesh.shape["sp"]
        self.heads = HEADS // self.cores


def core_total(values, lay):
    total = values.astype(BF16).astype(F32)
    for bit in bits_of(lay.cores):
        total = total + flip(total.astype(BF16), "dp", lay.cores, bit).astype(F32)
    return total


def core_part(values, axis, lay):
    share = values.shape[axis] // lay.cores
    return lax.dynamic_slice_in_dim(values, lax.axis_index("dp") * share, share, axis)


def heads_of(values, sequences, lay):
    return values.reshape(sequences, -1, lay.heads, HDIM)


def block_forward(inputs, modulation, weights, biases, stride, lay, beside=None):
    w_input, w_output, w_expand, w_reduce = weights
    query_bias, value_bias, output_bias, expand_bias, reduce_bias = biases
    groups, count, width = inputs.shape
    share = width // lay.cores
    shift_att, scale_att, gate_att, shift_mlp, scale_mlp, gate_mlp = jnp.split(
        modulation[:, None, :], 6, axis=-1
    )
    normed_att, inverse_att = layer_norm(inputs)
    attn_input = (normed_att * (1.0 + scale_att) + shift_att).astype(BF16)
    projected = project(attn_input, w_input)
    query = heads_of((projected[..., :share] + query_bias).astype(BF16), groups, lay)
    key = heads_of(projected[..., share : 2 * share].astype(BF16), groups, lay)
    value = heads_of((projected[..., 2 * share :] + value_bias).astype(BF16), groups, lay)
    mixed, logsum = attend(query, key, value, stride)
    attended = mixed.reshape(groups, count, share)
    branch = core_total(project_rows(attended, w_output), lay) + output_bias
    hidden = inputs + gate_att * branch
    if beside is not None:
        hidden = beside(hidden)
    normed_mlp, inverse_mlp = layer_norm(hidden)
    mlp_input = (normed_mlp * (1.0 + scale_mlp) + shift_mlp).astype(BF16)
    expanded = project(mlp_input, w_expand) + expand_bias
    activated = jax.nn.gelu(expanded, approximate=True).astype(BF16)
    reduced = core_total(project_rows(activated, w_reduce), lay) + reduce_bias
    output = hidden + gate_mlp * reduced
    kept = (
        normed_att,
        inverse_att,
        attn_input,
        query,
        key,
        value,
        attended,
        logsum,
        branch,
        normed_mlp,
        inverse_mlp,
        mlp_input,
        expanded,
        activated,
        reduced,
    )
    return (output, kept)


def block_backward(gradient, kept, modulation, weights, stride, lay, joint=False):
    w_input, w_output, w_expand, w_reduce = weights
    (
        normed_att,
        inverse_att,
        attn_input,
        query,
        key,
        value,
        attended,
        logsum,
        branch,
        normed_mlp,
        inverse_mlp,
        mlp_input,
        expanded,
        activated,
        reduced,
    ) = kept
    groups, count, width = gradient.shape
    share = width // lay.cores
    shift_att, scale_att, gate_att, shift_mlp, scale_mlp, gate_mlp = jnp.split(
        modulation[:, None, :], 6, axis=-1
    )
    grad_gate_mlp = jnp.sum(gradient * reduced, axis=1)
    grad_reduced = (gradient * gate_mlp).astype(BF16)
    columns = activated.shape[-1]
    if joint:
        reduce_grad = contract_first(flat(grad_reduced), flat(activated)).astype(BF16)
        reduce_grad, grad_reduced = tie([reduce_grad, grad_reduced], [])
    else:
        reduce_grad = contract_first(flat(grad_reduced), flat(activated)).astype(BF16)
    grad_activated = project(grad_reduced, w_reduce)
    gelu_back = jax.vjp(partial(jax.nn.gelu, approximate=True), expanded)[1]
    grad_expanded = gelu_back(grad_activated)[0].astype(BF16)
    if joint:
        joined = weight_grad(flat(mlp_input), flat(grad_expanded), 0, 2 * columns)
        joined, grad_expanded = tie([joined, grad_expanded], [])
    else:
        expand_grad = contract_first(flat(mlp_input), flat(grad_expanded)).astype(BF16)
    grad_mlp_input = core_total(project_rows(grad_expanded, w_expand), lay)
    grad_scale_mlp = jnp.sum(grad_mlp_input * normed_mlp, axis=1)
    grad_shift_mlp = jnp.sum(grad_mlp_input, axis=1)
    grad_hidden = gradient + norm_back(grad_mlp_input * (1.0 + scale_mlp), normed_mlp, inverse_mlp)
    grad_gate_att = jnp.sum(grad_hidden * branch, axis=1)
    grad_branch = (grad_hidden * gate_att).astype(BF16)
    grad_attended = project(grad_branch, w_output).astype(BF16)
    grad_query, grad_key, grad_value = attend_back(
        query, key, value, logsum, heads_of(grad_attended, groups, lay), stride
    )
    grad_query = grad_query.reshape(groups, count, share)
    grad_key = grad_key.reshape(groups, count, share)
    grad_value = grad_value.reshape(groups, count, share)
    grad_projected = jnp.concatenate([grad_query, grad_key, grad_value], axis=-1)
    left = jnp.concatenate([flat(attn_input), flat(grad_branch)], axis=0)
    right = jnp.concatenate(
        [
            jnp.pad(flat(grad_projected), ((0, 0), (0, share))),
            jnp.pad(flat(attended), ((0, 0), (3 * share, 0))),
        ],
        axis=0,
    )
    if joint:
        joined = weight_grad(left, right, columns, 2 * columns, joined)
    else:
        attention_grad = contract_first(left, right).astype(BF16)
    grad_attn_input = core_total(project_rows(grad_projected, w_input), lay)
    grad_scale_att = jnp.sum(grad_attn_input * normed_att, axis=1)
    grad_shift_att = jnp.sum(grad_attn_input, axis=1)
    grad_inputs = grad_hidden + norm_back(
        grad_attn_input * (1.0 + scale_att), normed_att, inverse_att
    )
    grad_mod = jnp.concatenate(
        [
            grad_shift_att,
            grad_scale_att,
            grad_gate_att,
            grad_shift_mlp,
            grad_scale_mlp,
            grad_gate_mlp,
        ],
        axis=-1,
    )
    split_biases = (token_sum(grad_query), token_sum(grad_value), token_sum(grad_expanded))
    whole_biases = (token_sum(grad_branch), token_sum(grad_reduced))
    return (
        grad_inputs,
        grad_mod,
        split_biases,
        whole_biases,
        (reduce_grad, joined) if joint else (attention_grad, expand_grad, reduce_grad),
    )


def shard_parts(w_input, w_output, w_expand, w_reduce, lay):
    rows = w_input.shape[0]
    attention = core_part(w_input.reshape(rows, 3, -1), 2, lay).reshape(rows, -1)
    return (
        attention,
        core_part(w_output, 1, lay),
        core_part(w_expand, 1, lay),
        core_part(w_reduce, 1, lay),
    )


def split_columns(values, widths):
    bounds = []
    offset = 0
    for width in widths[:-1]:
        offset = offset + width
        bounds.append(offset)
    return jnp.split(values, bounds, axis=-1)


def fetch_weights(gather, w_input, w_output, w_expand, w_reduce, lay):
    c_input, c_output, c_expand, c_reduce = shard_parts(w_input, w_output, w_expand, w_reduce, lay)
    attention = gather.chunk(jnp.concatenate([c_input, c_output], axis=1))
    expand = gather.chunk(c_expand)
    reduce = gather.chunk(c_reduce)
    count = c_input.shape[1]
    return (attention[:, :count], attention[:, count:], expand, reduce)


def fetch_whole(w_input, w_output, w_expand, w_reduce, lay):
    parts = shard_parts(w_input, w_output, w_expand, w_reduce, lay)
    whole = lax.all_gather(jnp.concatenate(parts, axis=1), "sp", axis=0, tiled=True)
    return split_columns(whole, [part.shape[1] for part in parts])


def reduce_joint(grads):
    g_reduce, g_joined = grads
    reduce = lax.psum_scatter(g_reduce, "sp", scatter_dimension=0, tiled=True)
    summed = lax.psum_scatter(g_joined, "sp", scatter_dimension=0, tiled=True)
    expand, attention = jnp.split(summed, 2, axis=1)
    return (attention, expand, reduce)


def reduce_weights(scatter, grads, first, second):
    g_attention, g_expand, g_reduce = grads
    reduce, _, _ = scatter.chunk(g_reduce)
    expand, _, _ = scatter.chunk(g_expand)
    attention, first, second = scatter.chunk(g_attention, first, second)
    return ((attention, expand, reduce), first, second)


def join_any(parts, lay):
    g_input, g_output, g_expand, g_reduce = [
        cube_gather(part.astype(BF16), "dp", lay.cores).astype(F32) for part in parts
    ]
    rows = g_output.shape[1]
    thirds = g_input.reshape(lay.cores, rows, 3, -1)
    return (
        jnp.transpose(thirds, (1, 2, 0, 3)).reshape(rows, -1),
        jnp.transpose(g_output, (1, 0, 2)).reshape(rows, -1),
        jnp.transpose(g_expand, (1, 0, 2)).reshape(rows, -1),
        jnp.transpose(g_reduce, (1, 0, 2)).reshape(rows, -1),
    )


def join_call(body, widths, own, other, name):
    rows = own.shape[0]
    return pl.pallas_call(
        body,
        out_shape=[jax.ShapeDtypeStruct((rows, width), F32) for width in widths],
        in_specs=[pl.BlockSpec(memory_space=pltpu.VMEM)] * 2,
        out_specs=[pl.BlockSpec(memory_space=pltpu.VMEM)] * len(widths),
        compiler_params=pltpu.CompilerParams(vmem_limit_bytes=24 << 20),
        cost_estimate=pl.CostEstimate(
            flops=0, transcendentals=0, bytes_accessed=2 * rows * sum(widths) * 4
        ),
        name=name,
    )(own, other)


def in_order(write):
    core = lax.axis_index("dp")
    for first in (0, 1):
        pl.when(core == first)(partial(write, first, 1 - first))


def join_pair(own):
    own = own.astype(BF16)
    columns = own.shape[1]

    def body(own_ref, other_ref, out_ref):
        def write(low, high):
            refs = (own_ref, other_ref)
            out_ref[:, :columns] = refs[low][...].astype(F32)
            out_ref[:, columns:] = refs[high][...].astype(F32)

        in_order(write)

    return join_call(body, [2 * columns], own, flip(own, "dp", 2, 1), "join_pair")[0]


def join_attention(own):
    own = own.astype(BF16)
    share = own.shape[1] // 4

    def body(own_ref, other_ref, in_ref, out_ref):
        def write(low, high):
            refs = (own_ref, other_ref)
            for place, which in ((0, low), (1, high)):
                values = refs[which][...].astype(F32)
                for k in range(3):
                    start = (2 * k + place) * share
                    in_ref[:, start : start + share] = values[:, k * share : (k + 1) * share]
                out_ref[:, place * share : (place + 1) * share] = values[:, 3 * share :]

        in_order(write)

    return join_call(body, [6 * share, 2 * share], own, flip(own, "dp", 2, 1), "join_attention")


def join_columns(sums, lay):
    attention, expand, reduce = sums
    if lay.cores == 2:
        g_input, g_output = join_attention(attention)
        return (g_input, g_output, join_pair(expand), join_pair(reduce))
    count = attention.shape[1] * 3 // 4
    return join_any((attention[:, :count], attention[:, count:], expand, reduce), lay)


def swap_chips(values):
    return lax.all_to_all(values, "sp", split_axis=0, concat_axis=0, tiled=True)


def to_positions(values, clips, lay):
    frames, patches, width = values.shape
    parts = jnp.transpose(
        values.reshape(frames, lay.chips, patches // lay.chips, width), (1, 0, 2, 3)
    )
    moved = swap_chips(parts.reshape(lay.chips, -1, width)).reshape(clips, -1, width)
    return cube_gather(moved, "dp", lay.cores).reshape(-1, moved.shape[1], width)


def own_group(values, lay):
    share = values.shape[0] // lay.cores
    return lax.dynamic_slice_in_dim(values, lax.axis_index("dp") * share, share, 0)


def to_frames(values, frames_here, lay):
    own = own_group(values, lay)
    width = own.shape[-1]
    moved = swap_chips(own.reshape(lay.chips, -1, width))
    parts = jnp.transpose(moved.reshape(lay.chips, frames_here, -1, width), (1, 0, 2, 3))
    return parts.reshape(frames_here, -1, width)


def place_split(values, lay):
    whole = jnp.zeros((lay.cores,) + values.shape, values.dtype)
    whole = lax.dynamic_update_index_in_dim(whole, values, lax.axis_index("dp"), 0)
    return whole.reshape(-1)


def per_device(
    lay,
    frames,
    cotangent,
    aspect,
    table_index,
    noise_level,
    labels,
    row_table,
    column_table,
    class_table,
    time_first,
    time_first_bias,
    time_second,
    time_second_bias,
    modulate,
    modulate_bias,
    spatial_input,
    spatial_input_bias,
    spatial_output,
    spatial_output_bias,
    spatial_expand,
    spatial_expand_bias,
    spatial_reduce,
    spatial_reduce_bias,
    temporal_input,
    temporal_input_bias,
    temporal_output,
    temporal_output_bias,
    temporal_expand,
    temporal_expand_bias,
    temporal_reduce,
    temporal_reduce_bias,
):
    cores, chips = lay.cores, lay.chips
    chip = lax.axis_index("sp")
    core = lax.axis_index("dp")
    frame_count, patches, width = frames.shape
    clips_here = aspect.shape[0]
    clips = cores * clips_here
    clip_here = chip * frame_count // FRAMES

    gather = Gather(lay)
    scatter = Scatter(lay)
    spatial_weights = fetch_weights(
        gather, spatial_input, spatial_output, spatial_expand, spatial_reduce, lay
    )
    temporal_weights = fetch_whole(
        temporal_input, temporal_output, temporal_expand, temporal_reduce, lay
    )

    facts = cube_gather(jnp.stack([aspect, table_index, noise_level, labels]), "dp", cores)
    group_aspect, group_table = (
        lax.dynamic_index_in_dim(facts[:, k], clip_here, 1, keepdims=False) for k in (0, 1)
    )
    all_levels = facts[:, 2].reshape(clips)
    all_labels = facts[:, 3].reshape(clips)
    group_clips = jnp.arange(cores) * clips_here + clip_here

    half = FREQ // 2
    frequency = jnp.exp(-math.log(10000.0) * jnp.arange(half, dtype=F32) / half)
    angles = all_levels.astype(F32)[:, None] * frequency[None, :]
    embedding = jnp.concatenate([jnp.cos(angles), jnp.sin(angles)], axis=-1).astype(BF16)
    time_hidden = project(embedding, time_first) + time_first_bias.astype(F32)
    time_act = jax.nn.silu(time_hidden).astype(BF16)
    class_pick = (all_labels[:, None] == lax.iota(jnp.int32, class_table.shape[0])[None, :]).astype(
        BF16
    )
    condition = (
        project(time_act, time_second)
        + time_second_bias.astype(F32)
        + project(class_pick, class_table)
    )
    condition_act = jax.nn.silu(condition).astype(BF16)
    mod_cols = project(condition_act, modulate) + modulate_bias.astype(F32)

    bias_shards = (
        spatial_input_bias,
        spatial_output_bias,
        spatial_expand_bias,
        spatial_reduce_bias,
        temporal_input_bias,
        temporal_output_bias,
        temporal_expand_bias,
        temporal_reduce_bias,
    )
    bias_sizes = [shard.shape[0] for shard in bias_shards]
    small = jnp.concatenate([mod_cols.reshape(-1)] + [shard.astype(F32) for shard in bias_shards])
    gathered = cube_gather(small, "sp", chips)
    mod_size = mod_cols.shape[1]
    pieces = split_columns(gathered, [clips * mod_size] + bias_sizes)
    modulation = jnp.transpose(pieces[0].reshape(chips, clips, mod_size), (1, 0, 2)).reshape(
        clips, chips * mod_size
    )
    whole_biases = [piece.reshape(-1) for piece in pieces[1:]]

    def block_biases(parts):
        query_bias, value_bias = jnp.split(parts[0], 2)
        return (
            core_part(query_bias, 0, lay),
            core_part(value_bias, 0, lay),
            parts[1],
            core_part(parts[2], 0, lay),
            parts[3],
        )

    spatial_biases = block_biases(whole_biases[:4])
    temporal_biases = block_biases(whole_biases[4:])
    clip_pick = (group_clips[:, None] == jnp.arange(clips)[None, :]).astype(F32)
    spatial_mod = jnp.sum(
        clip_pick[:, :, None] * modulation[None, :, : 6 * width], axis=1
    )
    temporal_mod = modulation[:, 6 * width :]

    row_width = jnp.where(
        group_aspect == 0, SIDE, jnp.where(group_aspect == 1, 2 * SIDE, SIDE // 2)
    )[:, None, None]
    patch_ids = lax.iota(jnp.int32, patches)[None, :, None]
    grid_ids = lax.iota(jnp.int32, 2 * SIDE)[None, None, :]
    row_pick = (patch_ids // row_width == grid_ids).astype(BF16)
    col_pick = (patch_ids % row_width == grid_ids).astype(BF16)
    row_chosen = jnp.take(row_table, group_table, axis=0)
    col_chosen = jnp.take(column_table, group_table, axis=0)
    positions = jnp.einsum(
        "gpr,grd->gpd", row_pick, row_chosen, preferred_element_type=F32
    ) + jnp.einsum("gpr,grd->gpd", col_pick, col_chosen, preferred_element_type=F32)
    all_frames = cube_gather(frames, "dp", cores).astype(F32)
    block_input = (all_frames + positions[:, None]).reshape(-1, patches, width)
    frame_mod = jnp.repeat(spatial_mod, frame_count, axis=0)

    exchanged_after = []

    def exchange_cotangent(hidden):
        hidden, moving = tie([hidden, cotangent], [])
        hidden, moved = tie([hidden, to_positions(moving, clips_here, lay)], [])
        exchanged_after.append(moved)
        return hidden

    spatial_out, spatial_kept = block_forward(
        block_input, frame_mod, spatial_weights, spatial_biases, 1, lay, exchange_cotangent
    )
    grad_after = exchanged_after[0]
    own_out = own_group(spatial_out.astype(BF16), lay)
    between = to_positions(own_out, clips_here, lay)
    local_patches = patches // chips
    temporal_out, temporal_kept = block_forward(
        between.astype(F32), temporal_mod, temporal_weights, temporal_biases, local_patches, lay
    )
    grad_between, temporal_dmod, temporal_split, temporal_whole, temporal_grads = block_backward(
        grad_after.astype(F32), temporal_kept, temporal_mod, temporal_weights, local_patches, lay, True
    )
    temporal_sums = reduce_joint(temporal_grads)
    own_grad = to_frames(grad_between.astype(BF16), frame_count, lay)
    grad_frames = cube_gather(own_grad, "dp", cores).reshape(-1, patches, width)
    input_grad_all, frame_dmod, spatial_split, spatial_whole, spatial_grads = block_backward(
        grad_frames.astype(F32), spatial_kept, frame_mod, spatial_weights, 1, lay
    )
    reduce_sums, input_grad_all, temporal_low = tie([temporal_sums[2], input_grad_all, temporal_out.astype(BF16)], [])
    temporal_sums = temporal_sums[:2] + (reduce_sums,)
    activations = to_frames(temporal_low, frame_count, lay)
    input_grad = own_group(input_grad_all, lay)

    grad_positions = jnp.sum(input_grad, axis=0)
    own_rows = lax.dynamic_index_in_dim(row_pick, core, 0, keepdims=False).astype(F32)
    own_cols = lax.dynamic_index_in_dim(col_pick, core, 0, keepdims=False).astype(F32)
    table_part = contract_first(
        jnp.concatenate([own_rows, own_cols], axis=1), grad_positions, HIGHEST
    )
    here = (lax.iota(jnp.int32, clips_here) == clip_here).astype(F32)
    table_part = here[:, None, None] * table_part[None]

    spatial_dmod = jnp.sum(frame_dmod.reshape(cores, frame_count, -1), axis=1)
    spatial_dmod = jnp.sum(clip_pick[:, :, None] * spatial_dmod[:, None, :], axis=0)
    grad_mod = jnp.concatenate([spatial_dmod, temporal_dmod], axis=-1)

    def by_chip(values):
        parts = values.reshape(-1, chips, values.shape[-1] // chips)
        return jnp.transpose(parts, (1, 0, 2)).reshape(chips, -1)

    def bias_rows(split, whole):
        query_sum, value_sum, expand_sum = [place_split(part, lay) for part in split]
        output_sum, reduce_sum = whole
        return (
            by_chip(jnp.concatenate([query_sum, value_sum])),
            by_chip(expand_sum),
            by_chip(output_sum),
            by_chip(reduce_sum),
        )

    spatial_rows = bias_rows(spatial_split, spatial_whole)
    temporal_rows = bias_rows(temporal_split, temporal_whole)
    rows = (
        by_chip(table_part.reshape(-1, width)),
        spatial_rows[0],
        spatial_rows[1],
        temporal_rows[0],
        temporal_rows[1],
        by_chip(grad_mod),
        spatial_rows[2],
        spatial_rows[3],
        temporal_rows[2],
        temporal_rows[3],
    )
    summed = cube_scatter(jnp.concatenate(rows, axis=1), "sp", chips)
    spatial_sums, ready_first, ready_second = reduce_weights(
        scatter, spatial_grads, [], []
    )
    sums = split_columns(summed, [row.shape[1] for row in rows])

    mod_low = sums[5].reshape(clips, -1).astype(BF16)
    modulate_bias_grad = jnp.sum(mod_low.astype(F32), axis=0)
    modulate_grad = contract_first(condition_act, mod_low)
    condition_part = project_rows(mod_low, modulate)

    table_sum = sums[0].reshape(clips_here, -1)
    table_pick = (lax.iota(jnp.int32, row_table.shape[0])[:, None] == table_index[None, :]).astype(
        F32
    )
    table_placed = jnp.sum(table_pick[:, :, None] * table_sum[None], axis=1)
    exchanged = jnp.concatenate([table_placed.reshape(-1)] + [sums[k] for k in (1, 2, 3, 4)])
    exchanged = cube_sum(exchanged, "dp", cores)
    tables, s_input_bias, s_expand_bias, t_input_bias, t_expand_bias = split_columns(
        exchanged, [table_placed.size] + [sums[k].shape[0] for k in (1, 2, 3, 4)]
    )
    tables = tables.reshape(row_table.shape[0], 2, 2 * SIDE, -1)

    grad_condition_act = cube_sum(condition_part, "sp", chips)
    silu_back = jax.vjp(jax.nn.silu, condition)[1]
    grad_condition = silu_back(grad_condition_act)[0]
    class_grad = contract_first(class_pick.astype(F32), grad_condition, HIGHEST)
    grad_time = grad_condition.astype(BF16)
    time_second_bias_grad = jnp.sum(grad_time.astype(F32), axis=0)
    time_second_grad = contract_first(time_act, grad_time)
    grad_time_act = project_rows(grad_time, time_second)
    time_silu_back = jax.vjp(jax.nn.silu, time_hidden)[1]
    grad_time_hidden = time_silu_back(grad_time_act)[0].astype(BF16)
    time_first_bias_grad = jnp.sum(grad_time_hidden.astype(F32), axis=0)
    time_first_grad = contract_first(embedding, grad_time_hidden)

    s_input, s_output, s_expand, s_reduce = join_columns(spatial_sums, lay)
    t_input, t_output, t_expand, t_reduce = join_columns(temporal_sums, lay)
    return (
        activations,
        input_grad,
        tables[:, 0],
        tables[:, 1],
        class_grad,
        time_first_grad,
        time_first_bias_grad,
        time_second_grad,
        time_second_bias_grad,
        modulate_grad,
        modulate_bias_grad,
        s_input,
        s_input_bias,
        s_output,
        sums[6],
        s_expand,
        s_expand_bias,
        s_reduce,
        sums[7],
        t_input,
        t_input_bias,
        t_output,
        sums[8],
        t_expand,
        t_expand_bias,
        t_reduce,
        sums[9],
    )


def solution(mesh):
    in_specs = (
        P(("dp", "sp"), None, None),
        P(("dp", "sp"), None, None),
        P("dp"),
        P("dp"),
        P("dp"),
        P("dp"),
        P(),
        P(),
        P(),
        P(),
        P(),
        P(),
        P(),
        P(None, "sp"),
        P("sp"),
        P("sp", None),
        P("sp"),
        P("sp", None),
        P("sp"),
        P("sp", None),
        P("sp"),
        P("sp", None),
        P("sp"),
        P("sp", None),
        P("sp"),
        P("sp", None),
        P("sp"),
        P("sp", None),
        P("sp"),
        P("sp", None),
        P("sp"),
    )
    out_specs = (
        P(("dp", "sp"), None, None),
        P(("dp", "sp"), None, None),
        P(None, None, "sp"),
        P(None, None, "sp"),
        P(),
        P(),
        P(),
        P(),
        P(),
        P(None, "sp"),
        P("sp"),
        P("sp", None),
        P("sp"),
        P("sp", None),
        P("sp"),
        P("sp", None),
        P("sp"),
        P("sp", None),
        P("sp"),
        P("sp", None),
        P("sp"),
        P("sp", None),
        P("sp"),
        P("sp", None),
        P("sp"),
        P("sp", None),
        P("sp"),
    )
    return jax.shard_map(
        partial(per_device, Layout(mesh)), mesh=mesh, in_specs=in_specs, out_specs=out_specs, check_vma=False
    )
```

```python
from functools import partial
import math

import jax
import jax.numpy as jnp
from jax import lax
from jax.experimental import pallas as pl
from jax.experimental.pallas import tpu as pltpu
from jax.sharding import PartitionSpec as P

HEADS = 16
HDIM = 72
FREQ = 256
SIDE = 16
FRAMES = 16

EPSILON = 1e-06
HIGHEST = lax.Precision.HIGHEST
BF16 = jnp.bfloat16
F32 = jnp.float32


def layer_norm(values):
    center = values - jnp.mean(values, axis=-1, keepdims=True)
    inverse = lax.rsqrt(jnp.mean(center * center, axis=-1, keepdims=True) + EPSILON)
    return (center * inverse, inverse)


def norm_back(gradient, normed, inverse):
    mean_grad = jnp.mean(gradient, axis=-1, keepdims=True)
    mean_cross = jnp.mean(gradient * normed, axis=-1, keepdims=True)
    return inverse * (gradient - mean_grad - normed * mean_cross)


def project(left_rows, weight):
    return lax.dot_general(
        left_rows,
        weight,
        (((left_rows.ndim - 1,), (0,)), ((), ())),
        preferred_element_type=F32,
    )


def project_rows(left_rows, weight):
    return lax.dot_general(
        left_rows,
        weight,
        (((left_rows.ndim - 1,), (1,)), ((), ())),
        preferred_element_type=F32,
    )


def contract_first(left_rows, right_rows, precision=None):
    return lax.dot_general(
        left_rows,
        right_rows,
        (((0,), (0,)), ((), ())),
        preferred_element_type=F32,
        precision=precision,
    )


def flat(values):
    return values.reshape(-1, values.shape[-1])


def token_sum(values):
    return jnp.sum(flat(values).astype(F32), axis=0)


def flip(values, axis, size, bit):
    return lax.ppermute(values, axis, [(i, i ^ bit) for i in range(size)])


def bits_of(size):
    bits = []
    bit = 1
    while bit < size:
        bits.append(bit)
        bit = bit * 2
    assert bit == size
    return bits


def cube_gather(values, axis, size):
    rank = lax.axis_index(axis)
    held = values[None]
    for bit in bits_of(size):
        other = flip(held, axis, size, bit)
        upper = (rank & bit) != 0
        held = jnp.concatenate(
            [jnp.where(upper, other, held), jnp.where(upper, held, other)], axis=0
        )
    return held


def cube_sum(values, axis, size):
    for bit in bits_of(size):
        values = values + flip(values, axis, size, bit)
    return values


def cube_scatter(values, axis, size):
    rank = lax.axis_index(axis)
    for bit in bits_of(size):
        upper = (rank & bit) != 0
        pairs = values.reshape((-1, 2) + values.shape[1:])
        low, high = pairs[:, 0], pairs[:, 1]
        away = jnp.where(upper, low, high)
        kept = jnp.where(upper, high, low)
        values = kept + flip(away, axis, size, bit)
    return values[0]


def tie(values, others):
    values = list(values)
    return lax.optimization_barrier(tuple(values) + tuple(others))[: len(values)]


def pick(values, axis, index):
    return lax.dynamic_index_in_dim(values, index, axis, keepdims=False)


def add_low(left, right):
    return (left.astype(F32) + right.astype(F32)).astype(BF16)


def hop(values, lay, bit):
    return flip(values, "sp", lay.chips, bit)


def turn(values, lay, offset):
    count = lay.chips
    return lax.ppermute(values, "sp", [(i, (i + 4 * offset) % count) for i in range(count)])


def put_kernel(depth, cut, held_ref, x_ref, y_ref, low_ref, high_ref, out_ref):
    chip = lax.axis_index("sp")
    z, y, x = chip // 4, lax.rem(chip // 2, 2), lax.rem(chip, 2)
    for k in range(depth):
        layer = lax.rem(z + depth - k, depth)
        out_ref[layer, y, x] = held_ref[k]
        out_ref[layer, y, 1 - x] = x_ref[k]
        out_ref[layer, 1 - y, x] = y_ref[k]
        out_ref[layer, 1 - y, 1 - x, :, :cut] = low_ref[k]
        out_ref[layer, 1 - y, 1 - x, :, cut:] = high_ref[k]


def put_rows(arrays, cut):
    depth, rows, columns = arrays[0].shape
    whole = pl.pallas_call(
        partial(put_kernel, depth, cut),
        out_shape=jax.ShapeDtypeStruct((depth, 2, 2, rows, columns), BF16),
        in_specs=[pl.BlockSpec(memory_space=pltpu.VMEM)] * 5,
        out_specs=pl.BlockSpec(memory_space=pltpu.VMEM),
        compiler_params=pltpu.CompilerParams(vmem_limit_bytes=24 << 20),
        cost_estimate=pl.CostEstimate(
            flops=0, transcendentals=0, bytes_accessed=16 * depth * rows * columns
        ),
        name="put_rows",
    )(*arrays)
    return whole.reshape(depth * 4 * rows, columns)


def cut_of(columns):
    return columns // 256 * 128


class Gather:
    def __init__(self, lay):
        self.lay = lay
        self.layers = []
        self.sides = []
        self.corners = []

    def chunk(self, shard):
        lay = self.lay
        cut = cut_of(shard.shape[1])
        after = (self.layers[-1] if self.layers else []) + (
            self.corners[-2] if len(self.corners) > 1 else []
        )
        if after:
            (shard,) = tie([shard], after)
        layers = [turn(shard, lay, k) for k in range(1, lay.chips // 4)]
        held = jnp.stack([shard] + layers)
        if self.sides:
            (held,) = tie([held], self.sides[-1])
        along_x, along_y = hop(held, lay, 1), hop(held, lay, 2)
        low = hop(along_x[:, :, :cut], lay, 2)
        high = hop(along_y[:, :, cut:], lay, 1)
        self.layers.append(layers)
        self.sides.append([along_x, along_y])
        self.corners.append([low, high])
        return put_rows([held, along_x, along_y, low, high], cut)


class Scatter:
    def __init__(self, lay):
        self.lay = lay
        self.layers = []
        self.sides = []
        self.corners = []

    def chunk(self, grad, first=(), second=()):
        lay = self.lay
        depth = lay.chips // 4
        chip = lax.axis_index("sp")
        z, y, x = chip // 4, (chip // 2) % 2, chip % 2
        cut = cut_of(grad.shape[1])
        grid = grad.reshape(depth, 2, 2, -1, grad.shape[1])

        def at(row, column):
            return pick(pick(grid, 1, row), 1, column)

        corner = at(1 - y, 1 - x)
        low, high = corner[..., :cut], corner[..., cut:]
        after = (self.corners[-1] if self.corners else []) + (
            self.sides[-2] if len(self.sides) > 1 else []
        )
        if after:
            low, high = tie([low, high], after)
        low_got, high_got = hop(low, lay, 2), hop(high, lay, 1)
        side_x, side_y = at(y, 1 - x), at(1 - y, x)
        send_x = jnp.concatenate([add_low(side_x[..., :cut], low_got), side_x[..., cut:]], axis=-1)
        send_y = jnp.concatenate([side_y[..., :cut], add_low(side_y[..., cut:], high_got)], axis=-1)
        if len(self.layers) > 1:
            send_x, send_y = tie([send_x, send_y], self.layers[-2])
        got_x, got_y = hop(send_x, lay, 1), hop(send_y, lay, 2)
        own = at(y, x)
        got_x, got_y, *first = tie([got_x, got_y] + list(first), [])

        def part(layer):
            return (
                pick(own, 0, layer).astype(F32)
                + pick(got_x, 0, layer).astype(F32)
                + pick(got_y, 0, layer).astype(F32)
            )

        layers = [turn(part((z + k) % depth).astype(BF16), lay, k) for k in range(1, depth)]
        tied = tie(list(layers) + list(second), [])
        layers, second = tied[: depth - 1], tied[depth - 1 :]
        total = part(z)
        for got in layers:
            total = total + got.astype(F32)
        self.layers.append(layers)
        self.sides.append([got_x, got_y])
        self.corners.append([low_got, high_got])
        return (total, list(first), list(second))


def tile_of(columns):
    for tile in (384, 256, 128):
        if columns % tile == 0:
            return tile
    return columns


def fixed_spec(array):
    return pl.BlockSpec(array.shape, lambda j: (0, 0))


def weight_grad(left, right, offset, total, joined=None):
    depth, rows = left.shape
    columns = right.shape[1]
    tile = tile_of(math.gcd(columns, offset) if offset else columns)
    skip = offset // tile

    def body(left_ref, right_ref, *refs):
        out_ref, turned_ref = refs[-2:]

        @pl.when(pl.program_id(0) == 0)
        def _():
            turned_ref[...] = left_ref[...].T

        out_ref[...] = jnp.dot(
            turned_ref[...], right_ref[...], preferred_element_type=F32
        ).astype(BF16)

    held = [] if joined is None else [joined]
    return pl.pallas_call(
        body,
        grid=(columns // tile,),
        in_specs=[fixed_spec(left), pl.BlockSpec((depth, tile), lambda j: (0, j))]
        + [pl.BlockSpec(memory_space=pl.ANY)] * len(held),
        out_specs=pl.BlockSpec((rows, tile), lambda j: (0, j + skip)),
        out_shape=jax.ShapeDtypeStruct((rows, total), BF16),
        scratch_shapes=[pltpu.VMEM((rows, depth), BF16)],
        input_output_aliases={2: 0} if held else {},
        compiler_params=pltpu.CompilerParams(
            dimension_semantics=("arbitrary",), vmem_limit_bytes=40 << 20
        ),
        cost_estimate=pl.CostEstimate(
            flops=2 * depth * rows * columns,
            transcendentals=0,
            bytes_accessed=2 * (depth * rows + depth * columns + rows * columns),
        ),
        name="weight_grad",
    )(left, right, *held)


def attention_scores(query, key, stride):
    scores = jnp.einsum("snhd,smhd->shnm", query, key, preferred_element_type=F32)
    scores = scores * HDIM ** (-0.5)
    if stride > 1:
        count = scores.shape[-1]
        row = lax.broadcasted_iota(jnp.int32, (count, count), 0) % stride
        col = lax.broadcasted_iota(jnp.int32, (count, count), 1) % stride
        scores = jnp.where(row == col, scores, -1e30)
    return scores


def attend(query, key, value, stride):
    scores = attention_scores(query, key, stride)
    row_max = jnp.max(scores, axis=-1, keepdims=True)
    exponent = jnp.exp(scores - row_max)
    row_total = jnp.sum(exponent, axis=-1, keepdims=True)
    probs = (exponent / row_total).astype(BF16)
    mixed = jnp.einsum("shnm,smhd->snhd", probs, value, preferred_element_type=F32)
    return (mixed.astype(BF16), row_max + jnp.log(row_total))


def attend_back(query, key, value, logsum, grad_out, stride):
    scale = HDIM ** (-0.5)
    probs = jnp.exp(attention_scores(query, key, stride) - logsum)
    grad_probs = jnp.einsum("snhd,smhd->shnm", grad_out, value, preferred_element_type=F32)
    inner = jnp.sum(probs * grad_probs, axis=-1, keepdims=True)
    grad_scores = (probs * (grad_probs - inner)).astype(BF16)
    grad_query = (
        jnp.einsum("shnm,smhd->snhd", grad_scores, key, preferred_element_type=F32) * scale
    )
    grad_key = (
        jnp.einsum("shnm,snhd->smhd", grad_scores, query, preferred_element_type=F32) * scale
    )
    grad_value = jnp.einsum(
        "shnm,snhd->smhd", probs.astype(BF16), grad_out, preferred_element_type=F32
    )
    return (grad_query.astype(BF16), grad_key.astype(BF16), grad_value.astype(BF16))


class Layout:
    def __init__(self, mesh):
        self.cores = mesh.shape["dp"]
        self.chips = mesh.shape["sp"]
        self.heads = HEADS // self.cores


def core_total(values, lay):
    total = values.astype(BF16).astype(F32)
    for bit in bits_of(lay.cores):
        total = total + flip(total.astype(BF16), "dp", lay.cores, bit).astype(F32)
    return total


def core_part(values, axis, lay):
    share = values.shape[axis] // lay.cores
    return lax.dynamic_slice_in_dim(values, lax.axis_index("dp") * share, share, axis)


def heads_of(values, sequences, lay):
    return values.reshape(sequences, -1, lay.heads, HDIM)


def block_forward(inputs, modulation, weights, biases, stride, lay, beside=None):
    w_input, w_output, w_expand, w_reduce = weights
    query_bias, value_bias, output_bias, expand_bias, reduce_bias = biases
    groups, count, width = inputs.shape
    share = width // lay.cores
    shift_att, scale_att, gate_att, shift_mlp, scale_mlp, gate_mlp = jnp.split(
        modulation[:, None, :], 6, axis=-1
    )
    normed_att, inverse_att = layer_norm(inputs)
    attn_input = (normed_att * (1.0 + scale_att) + shift_att).astype(BF16)
    projected = project(attn_input, w_input)
    query = heads_of((projected[..., :share] + query_bias).astype(BF16), groups, lay)
    key = heads_of(projected[..., share : 2 * share].astype(BF16), groups, lay)
    value = heads_of((projected[..., 2 * share :] + value_bias).astype(BF16), groups, lay)
    mixed, logsum = attend(query, key, value, stride)
    attended = mixed.reshape(groups, count, share)
    branch = core_total(project_rows(attended, w_output), lay) + output_bias
    hidden = inputs + gate_att * branch
    if beside is not None:
        hidden = beside(hidden)
    normed_mlp, inverse_mlp = layer_norm(hidden)
    mlp_input = (normed_mlp * (1.0 + scale_mlp) + shift_mlp).astype(BF16)
    expanded = project(mlp_input, w_expand) + expand_bias
    activated = jax.nn.gelu(expanded, approximate=True).astype(BF16)
    reduced = core_total(project_rows(activated, w_reduce), lay) + reduce_bias
    output = hidden + gate_mlp * reduced
    kept = (
        normed_att,
        inverse_att,
        attn_input,
        query,
        key,
        value,
        attended,
        logsum,
        branch,
        normed_mlp,
        inverse_mlp,
        mlp_input,
        expanded,
        activated,
        reduced,
    )
    return (output, kept)


def block_backward(gradient, kept, modulation, weights, stride, lay, joint=False):
    w_input, w_output, w_expand, w_reduce = weights
    (
        normed_att,
        inverse_att,
        attn_input,
        query,
        key,
        value,
        attended,
        logsum,
        branch,
        normed_mlp,
        inverse_mlp,
        mlp_input,
        expanded,
        activated,
        reduced,
    ) = kept
    groups, count, width = gradient.shape
    share = width // lay.cores
    shift_att, scale_att, gate_att, shift_mlp, scale_mlp, gate_mlp = jnp.split(
        modulation[:, None, :], 6, axis=-1
    )
    grad_gate_mlp = jnp.sum(gradient * reduced, axis=1)
    grad_reduced = (gradient * gate_mlp).astype(BF16)
    columns = activated.shape[-1]
    if joint:
        reduce_grad = contract_first(flat(grad_reduced), flat(activated)).astype(BF16)
        reduce_grad, grad_reduced = tie([reduce_grad, grad_reduced], [])
    else:
        reduce_grad = contract_first(flat(grad_reduced), flat(activated)).astype(BF16)
    grad_activated = project(grad_reduced, w_reduce)
    gelu_back = jax.vjp(partial(jax.nn.gelu, approximate=True), expanded)[1]
    grad_expanded = gelu_back(grad_activated)[0].astype(BF16)
    if joint:
        joined = weight_grad(flat(mlp_input), flat(grad_expanded), 0, 2 * columns)
        joined, grad_expanded = tie([joined, grad_expanded], [])
    else:
        expand_grad = contract_first(flat(mlp_input), flat(grad_expanded)).astype(BF16)
    grad_mlp_input = core_total(project_rows(grad_expanded, w_expand), lay)
    grad_scale_mlp = jnp.sum(grad_mlp_input * normed_mlp, axis=1)
    grad_shift_mlp = jnp.sum(grad_mlp_input, axis=1)
    grad_hidden = gradient + norm_back(grad_mlp_input * (1.0 + scale_mlp), normed_mlp, inverse_mlp)
    grad_gate_att = jnp.sum(grad_hidden * branch, axis=1)
    grad_branch = (grad_hidden * gate_att).astype(BF16)
    grad_attended = project(grad_branch, w_output).astype(BF16)
    grad_query, grad_key, grad_value = attend_back(
        query, key, value, logsum, heads_of(grad_attended, groups, lay), stride
    )
    grad_query = grad_query.reshape(groups, count, share)
    grad_key = grad_key.reshape(groups, count, share)
    grad_value = grad_value.reshape(groups, count, share)
    grad_projected = jnp.concatenate([grad_query, grad_key, grad_value], axis=-1)
    left = jnp.concatenate([flat(attn_input), flat(grad_branch)], axis=0)
    right = jnp.concatenate(
        [
            jnp.pad(flat(grad_projected), ((0, 0), (0, share))),
            jnp.pad(flat(attended), ((0, 0), (3 * share, 0))),
        ],
        axis=0,
    )
    if joint:
        joined = weight_grad(left, right, columns, 2 * columns, joined)
    else:
        attention_grad = contract_first(left, right).astype(BF16)
    grad_attn_input = core_total(project_rows(grad_projected, w_input), lay)
    grad_scale_att = jnp.sum(grad_attn_input * normed_att, axis=1)
    grad_shift_att = jnp.sum(grad_attn_input, axis=1)
    grad_inputs = grad_hidden + norm_back(
        grad_attn_input * (1.0 + scale_att), normed_att, inverse_att
    )
    grad_mod = jnp.concatenate(
        [
            grad_shift_att,
            grad_scale_att,
            grad_gate_att,
            grad_shift_mlp,
            grad_scale_mlp,
            grad_gate_mlp,
        ],
        axis=-1,
    )
    split_biases = (token_sum(grad_query), token_sum(grad_value), token_sum(grad_expanded))
    whole_biases = (token_sum(grad_branch), token_sum(grad_reduced))
    return (
        grad_inputs,
        grad_mod,
        split_biases,
        whole_biases,
        (reduce_grad, joined) if joint else (attention_grad, expand_grad, reduce_grad),
    )


def shard_parts(w_input, w_output, w_expand, w_reduce, lay):
    rows = w_input.shape[0]
    attention = core_part(w_input.reshape(rows, 3, -1), 2, lay).reshape(rows, -1)
    return (
        attention,
        core_part(w_output, 1, lay),
        core_part(w_expand, 1, lay),
        core_part(w_reduce, 1, lay),
    )


def split_columns(values, widths):
    bounds = []
    offset = 0
    for width in widths[:-1]:
        offset = offset + width
        bounds.append(offset)
    return jnp.split(values, bounds, axis=-1)


def fetch_weights(gather, w_input, w_output, w_expand, w_reduce, lay):
    c_input, c_output, c_expand, c_reduce = shard_parts(w_input, w_output, w_expand, w_reduce, lay)
    attention = gather.chunk(jnp.concatenate([c_input, c_output], axis=1))
    expand = gather.chunk(c_expand)
    reduce = gather.chunk(c_reduce)
    count = c_input.shape[1]
    return (attention[:, :count], attention[:, count:], expand, reduce)


def fetch_whole(w_input, w_output, w_expand, w_reduce, lay):
    parts = shard_parts(w_input, w_output, w_expand, w_reduce, lay)
    whole = lax.all_gather(jnp.concatenate(parts, axis=1), "sp", axis=0, tiled=True)
    return split_columns(whole, [part.shape[1] for part in parts])


def reduce_joint(grads):
    g_reduce, g_joined = grads
    reduce = lax.psum_scatter(g_reduce, "sp", scatter_dimension=0, tiled=True)
    summed = lax.psum_scatter(g_joined, "sp", scatter_dimension=0, tiled=True)
    expand, attention = jnp.split(summed, 2, axis=1)
    return (attention, expand, reduce)


def reduce_weights(scatter, grads, first, second):
    g_attention, g_expand, g_reduce = grads
    reduce, _, _ = scatter.chunk(g_reduce)
    expand, _, _ = scatter.chunk(g_expand)
    attention, first, second = scatter.chunk(g_attention, first, second)
    return ((attention, expand, reduce), first, second)


def join_any(parts, lay):
    g_input, g_output, g_expand, g_reduce = [
        cube_gather(part.astype(BF16), "dp", lay.cores).astype(F32) for part in parts
    ]
    rows = g_output.shape[1]
    thirds = g_input.reshape(lay.cores, rows, 3, -1)
    return (
        jnp.transpose(thirds, (1, 2, 0, 3)).reshape(rows, -1),
        jnp.transpose(g_output, (1, 0, 2)).reshape(rows, -1),
        jnp.transpose(g_expand, (1, 0, 2)).reshape(rows, -1),
        jnp.transpose(g_reduce, (1, 0, 2)).reshape(rows, -1),
    )


def join_call(body, widths, own, other, name):
    rows = own.shape[0]
    return pl.pallas_call(
        body,
        out_shape=[jax.ShapeDtypeStruct((rows, width), F32) for width in widths],
        in_specs=[pl.BlockSpec(memory_space=pltpu.VMEM)] * 2,
        out_specs=[pl.BlockSpec(memory_space=pltpu.VMEM)] * len(widths),
        compiler_params=pltpu.CompilerParams(vmem_limit_bytes=24 << 20),
        cost_estimate=pl.CostEstimate(
            flops=0, transcendentals=0, bytes_accessed=2 * rows * sum(widths) * 4
        ),
        name=name,
    )(own, other)


def in_order(write):
    core = lax.axis_index("dp")
    for first in (0, 1):
        pl.when(core == first)(partial(write, first, 1 - first))


def join_pair(own):
    own = own.astype(BF16)
    columns = own.shape[1]

    def body(own_ref, other_ref, out_ref):
        def write(low, high):
            refs = (own_ref, other_ref)
            out_ref[:, :columns] = refs[low][...].astype(F32)
            out_ref[:, columns:] = refs[high][...].astype(F32)

        in_order(write)

    return join_call(body, [2 * columns], own, flip(own, "dp", 2, 1), "join_pair")[0]


def join_attention(own):
    own = own.astype(BF16)
    share = own.shape[1] // 4

    def body(own_ref, other_ref, in_ref, out_ref):
        def write(low, high):
            refs = (own_ref, other_ref)
            for place, which in ((0, low), (1, high)):
                values = refs[which][...].astype(F32)
                for k in range(3):
                    start = (2 * k + place) * share
                    in_ref[:, start : start + share] = values[:, k * share : (k + 1) * share]
                out_ref[:, place * share : (place + 1) * share] = values[:, 3 * share :]

        in_order(write)

    return join_call(body, [6 * share, 2 * share], own, flip(own, "dp", 2, 1), "join_attention")


def join_columns(sums, lay):
    attention, expand, reduce = sums
    if lay.cores == 2:
        g_input, g_output = join_attention(attention)
        return (g_input, g_output, join_pair(expand), join_pair(reduce))
    count = attention.shape[1] * 3 // 4
    return join_any((attention[:, :count], attention[:, count:], expand, reduce), lay)


def swap_chips(values):
    return lax.all_to_all(values, "sp", split_axis=0, concat_axis=0, tiled=True)


def to_positions(values, clips, lay):
    frames, patches, width = values.shape
    parts = jnp.transpose(
        values.reshape(frames, lay.chips, patches // lay.chips, width), (1, 0, 2, 3)
    )
    moved = swap_chips(parts.reshape(lay.chips, -1, width)).reshape(clips, -1, width)
    return cube_gather(moved, "dp", lay.cores).reshape(-1, moved.shape[1], width)


def own_group(values, lay):
    share = values.shape[0] // lay.cores
    return lax.dynamic_slice_in_dim(values, lax.axis_index("dp") * share, share, 0)


def to_frames(values, frames_here, lay):
    own = own_group(values, lay)
    width = own.shape[-1]
    moved = swap_chips(own.reshape(lay.chips, -1, width))
    parts = jnp.transpose(moved.reshape(lay.chips, frames_here, -1, width), (1, 0, 2, 3))
    return parts.reshape(frames_here, -1, width)


def place_split(values, lay):
    whole = jnp.zeros((lay.cores,) + values.shape, values.dtype)
    whole = lax.dynamic_update_index_in_dim(whole, values, lax.axis_index("dp"), 0)
    return whole.reshape(-1)


def per_device(
    lay,
    frames,
    cotangent,
    aspect,
    table_index,
    noise_level,
    labels,
    row_table,
    column_table,
    class_table,
    time_first,
    time_first_bias,
    time_second,
    time_second_bias,
    modulate,
    modulate_bias,
    spatial_input,
    spatial_input_bias,
    spatial_output,
    spatial_output_bias,
    spatial_expand,
    spatial_expand_bias,
    spatial_reduce,
    spatial_reduce_bias,
    temporal_input,
    temporal_input_bias,
    temporal_output,
    temporal_output_bias,
    temporal_expand,
    temporal_expand_bias,
    temporal_reduce,
    temporal_reduce_bias,
):
    cores, chips = lay.cores, lay.chips
    chip = lax.axis_index("sp")
    core = lax.axis_index("dp")
    frame_count, patches, width = frames.shape
    clips_here = aspect.shape[0]
    clips = cores * clips_here
    clip_here = chip * frame_count // FRAMES

    gather = Gather(lay)
    scatter = Scatter(lay)
    spatial_weights = fetch_weights(
        gather, spatial_input, spatial_output, spatial_expand, spatial_reduce, lay
    )
    temporal_weights = fetch_whole(
        temporal_input, temporal_output, temporal_expand, temporal_reduce, lay
    )

    facts = cube_gather(jnp.stack([aspect, table_index, noise_level, labels]), "dp", cores)
    group_aspect, group_table = (
        lax.dynamic_index_in_dim(facts[:, k], clip_here, 1, keepdims=False) for k in (0, 1)
    )
    all_levels = facts[:, 2].reshape(clips)
    all_labels = facts[:, 3].reshape(clips)
    group_clips = jnp.arange(cores) * clips_here + clip_here

    half = FREQ // 2
    frequency = jnp.exp(-math.log(10000.0) * jnp.arange(half, dtype=F32) / half)
    angles = all_levels.astype(F32)[:, None] * frequency[None, :]
    embedding = jnp.concatenate([jnp.cos(angles), jnp.sin(angles)], axis=-1).astype(BF16)
    time_hidden = project(embedding, time_first) + time_first_bias.astype(F32)
    time_act = jax.nn.silu(time_hidden).astype(BF16)
    class_pick = (all_labels[:, None] == lax.iota(jnp.int32, class_table.shape[0])[None, :]).astype(
        BF16
    )
    condition = (
        project(time_act, time_second)
        + time_second_bias.astype(F32)
        + project(class_pick, class_table)
    )
    condition_act = jax.nn.silu(condition).astype(BF16)
    mod_cols = project(condition_act, modulate) + modulate_bias.astype(F32)

    bias_shards = (
        spatial_input_bias,
        spatial_output_bias,
        spatial_expand_bias,
        spatial_reduce_bias,
        temporal_input_bias,
        temporal_output_bias,
        temporal_expand_bias,
        temporal_reduce_bias,
    )
    bias_sizes = [shard.shape[0] for shard in bias_shards]
    small = jnp.concatenate([mod_cols.reshape(-1)] + [shard.astype(F32) for shard in bias_shards])
    gathered = cube_gather(small, "sp", chips)
    mod_size = mod_cols.shape[1]
    pieces = split_columns(gathered, [clips * mod_size] + bias_sizes)
    modulation = jnp.transpose(pieces[0].reshape(chips, clips, mod_size), (1, 0, 2)).reshape(
        clips, chips * mod_size
    )
    whole_biases = [piece.reshape(-1) for piece in pieces[1:]]

    def block_biases(parts):
        query_bias, value_bias = jnp.split(parts[0], 2)
        return (
            core_part(query_bias, 0, lay),
            core_part(value_bias, 0, lay),
            parts[1],
            core_part(parts[2], 0, lay),
            parts[3],
        )

    spatial_biases = block_biases(whole_biases[:4])
    temporal_biases = block_biases(whole_biases[4:])
    clip_pick = (group_clips[:, None] == jnp.arange(clips)[None, :]).astype(F32)
    spatial_mod = jnp.sum(
        clip_pick[:, :, None] * modulation[None, :, : 6 * width], axis=1
    )
    temporal_mod = modulation[:, 6 * width :]

    row_width = jnp.where(
        group_aspect == 0, SIDE, jnp.where(group_aspect == 1, 2 * SIDE, SIDE // 2)
    )[:, None, None]
    patch_ids = lax.iota(jnp.int32, patches)[None, :, None]
    grid_ids = lax.iota(jnp.int32, 2 * SIDE)[None, None, :]
    row_pick = (patch_ids // row_width == grid_ids).astype(BF16)
    col_pick = (patch_ids % row_width == grid_ids).astype(BF16)
    row_chosen = jnp.take(row_table, group_table, axis=0)
    col_chosen = jnp.take(column_table, group_table, axis=0)
    positions = jnp.einsum(
        "gpr,grd->gpd", row_pick, row_chosen, preferred_element_type=F32
    ) + jnp.einsum("gpr,grd->gpd", col_pick, col_chosen, preferred_element_type=F32)
    all_frames = cube_gather(frames, "dp", cores).astype(F32)
    block_input = (all_frames + positions[:, None]).reshape(-1, patches, width)
    frame_mod = jnp.repeat(spatial_mod, frame_count, axis=0)

    exchanged_after = []

    def exchange_cotangent(hidden):
        hidden, moving = tie([hidden, cotangent], [])
        hidden, moved = tie([hidden, to_positions(moving, clips_here, lay)], [])
        exchanged_after.append(moved)
        return hidden

    spatial_out, spatial_kept = block_forward(
        block_input, frame_mod, spatial_weights, spatial_biases, 1, lay, exchange_cotangent
    )
    grad_after = exchanged_after[0]
    own_out = own_group(spatial_out.astype(BF16), lay)
    between = to_positions(own_out, clips_here, lay)
    local_patches = patches // chips
    temporal_out, temporal_kept = block_forward(
        between.astype(F32), temporal_mod, temporal_weights, temporal_biases, local_patches, lay
    )
    grad_between, temporal_dmod, temporal_split, temporal_whole, temporal_grads = block_backward(
        grad_after.astype(F32), temporal_kept, temporal_mod, temporal_weights, local_patches, lay, True
    )
    temporal_sums = reduce_joint(temporal_grads)
    own_grad = to_frames(grad_between.astype(BF16), frame_count, lay)
    grad_frames = cube_gather(own_grad, "dp", cores).reshape(-1, patches, width)
    input_grad_all, frame_dmod, spatial_split, spatial_whole, spatial_grads = block_backward(
        grad_frames.astype(F32), spatial_kept, frame_mod, spatial_weights, 1, lay
    )
    reduce_sums, input_grad_all, temporal_low = tie([temporal_sums[2], input_grad_all, temporal_out.astype(BF16)], [])
    temporal_sums = temporal_sums[:2] + (reduce_sums,)
    activations = to_frames(temporal_low, frame_count, lay)
    input_grad = own_group(input_grad_all, lay)

    grad_positions = jnp.sum(input_grad, axis=0)
    own_rows = lax.dynamic_index_in_dim(row_pick, core, 0, keepdims=False).astype(F32)
    own_cols = lax.dynamic_index_in_dim(col_pick, core, 0, keepdims=False).astype(F32)
    table_part = contract_first(
        jnp.concatenate([own_rows, own_cols], axis=1), grad_positions, HIGHEST
    )
    here = (lax.iota(jnp.int32, clips_here) == clip_here).astype(F32)
    table_part = here[:, None, None] * table_part[None]

    spatial_dmod = jnp.sum(frame_dmod.reshape(cores, frame_count, -1), axis=1)
    spatial_dmod = jnp.sum(clip_pick[:, :, None] * spatial_dmod[:, None, :], axis=0)
    grad_mod = jnp.concatenate([spatial_dmod, temporal_dmod], axis=-1)

    def by_chip(values):
        parts = values.reshape(-1, chips, values.shape[-1] // chips)
        return jnp.transpose(parts, (1, 0, 2)).reshape(chips, -1)

    def bias_rows(split, whole):
        query_sum, value_sum, expand_sum = [place_split(part, lay) for part in split]
        output_sum, reduce_sum = whole
        return (
            by_chip(jnp.concatenate([query_sum, value_sum])),
            by_chip(expand_sum),
            by_chip(output_sum),
            by_chip(reduce_sum),
        )

    spatial_rows = bias_rows(spatial_split, spatial_whole)
    temporal_rows = bias_rows(temporal_split, temporal_whole)
    rows = (
        by_chip(table_part.reshape(-1, width)),
        spatial_rows[0],
        spatial_rows[1],
        temporal_rows[0],
        temporal_rows[1],
        by_chip(grad_mod),
        spatial_rows[2],
        spatial_rows[3],
        temporal_rows[2],
        temporal_rows[3],
    )
    summed = cube_scatter(jnp.concatenate(rows, axis=1), "sp", chips)
    spatial_sums, ready_first, ready_second = reduce_weights(
        scatter, spatial_grads, [], []
    )
    sums = split_columns(summed, [row.shape[1] for row in rows])

    mod_low = sums[5].reshape(clips, -1).astype(BF16)
    modulate_bias_grad = jnp.sum(mod_low.astype(F32), axis=0)
    modulate_grad = contract_first(condition_act, mod_low)
    condition_part = project_rows(mod_low, modulate)

    table_sum = sums[0].reshape(clips_here, -1)
    table_pick = (lax.iota(jnp.int32, row_table.shape[0])[:, None] == table_index[None, :]).astype(
        F32
    )
    table_placed = jnp.sum(table_pick[:, :, None] * table_sum[None], axis=1)
    exchanged = jnp.concatenate([table_placed.reshape(-1)] + [sums[k] for k in (1, 2, 3, 4)])
    exchanged = cube_sum(exchanged, "dp", cores)
    tables, s_input_bias, s_expand_bias, t_input_bias, t_expand_bias = split_columns(
        exchanged, [table_placed.size] + [sums[k].shape[0] for k in (1, 2, 3, 4)]
    )
    tables = tables.reshape(row_table.shape[0], 2, 2 * SIDE, -1)

    grad_condition_act = cube_sum(condition_part, "sp", chips)
    silu_back = jax.vjp(jax.nn.silu, condition)[1]
    grad_condition = silu_back(grad_condition_act)[0]
    class_grad = contract_first(class_pick.astype(F32), grad_condition, HIGHEST)
    grad_time = grad_condition.astype(BF16)
    time_second_bias_grad = jnp.sum(grad_time.astype(F32), axis=0)
    time_second_grad = contract_first(time_act, grad_time)
    grad_time_act = project_rows(grad_time, time_second)
    time_silu_back = jax.vjp(jax.nn.silu, time_hidden)[1]
    grad_time_hidden = time_silu_back(grad_time_act)[0].astype(BF16)
    time_first_bias_grad = jnp.sum(grad_time_hidden.astype(F32), axis=0)
    time_first_grad = contract_first(embedding, grad_time_hidden)

    s_input, s_output, s_expand, s_reduce = join_columns(spatial_sums, lay)
    t_input, t_output, t_expand, t_reduce = join_columns(temporal_sums, lay)
    return (
        activations,
        input_grad,
        tables[:, 0],
        tables[:, 1],
        class_grad,
        time_first_grad,
        time_first_bias_grad,
        time_second_grad,
        time_second_bias_grad,
        modulate_grad,
        modulate_bias_grad,
        s_input,
        s_input_bias,
        s_output,
        sums[6],
        s_expand,
        s_expand_bias,
        s_reduce,
        sums[7],
        t_input,
        t_input_bias,
        t_output,
        sums[8],
        t_expand,
        t_expand_bias,
        t_reduce,
        sums[9],
    )


def solution(mesh):
    in_specs = (
        P(("dp", "sp"), None, None),
        P(("dp", "sp"), None, None),
        P("dp"),
        P("dp"),
        P("dp"),
        P("dp"),
        P(),
        P(),
        P(),
        P(),
        P(),
        P(),
        P(),
        P(None, "sp"),
        P("sp"),
        P("sp", None),
        P("sp"),
        P("sp", None),
        P("sp"),
        P("sp", None),
        P("sp"),
        P("sp", None),
        P("sp"),
        P("sp", None),
        P("sp"),
        P("sp", None),
        P("sp"),
        P("sp", None),
        P("sp"),
        P("sp", None),
        P("sp"),
    )
    out_specs = (
        P(("dp", "sp"), None, None),
        P(("dp", "sp"), None, None),
        P(None, None, "sp"),
        P(None, None, "sp"),
        P(),
        P(),
        P(),
        P(),
        P(),
        P(None, "sp"),
        P("sp"),
        P("sp", None),
        P("sp"),
        P("sp", None),
        P("sp"),
        P("sp", None),
        P("sp"),
        P("sp", None),
        P("sp"),
        P("sp", None),
        P("sp"),
        P("sp", None),
        P("sp"),
        P("sp", None),
        P("sp"),
        P("sp", None),
        P("sp"),
    )
    return jax.shard_map(
        partial(per_device, Layout(mesh)), mesh=mesh, in_specs=in_specs, out_specs=out_specs, check_vma=False
    )
```
